32 devices in a mesh: dp: 8 (over y, x, core), grp: 4 (over z).
Axes of the slice: x: 2, y: 2, z: 4, core: 2. Of those that a mesh axis runs over, the one named last changes fastest.
Arguments:
- activations: bfloat16 [64, 14, 14, 512], P(('dp', 'grp')), may hold values from -6 to 6
- out_grads: bfloat16 [64, 14, 14, 512], P(('dp', 'grp')), may hold values from -60 to 60
- input_basis: bfloat16 [4608, 4608], P('grp'), may hold values from -0.09375 to 0.09375
- output_basis: bfloat16 [512, 512], replicated, may hold values from -0.25 to 0.25
- input_eigen: float32 [4608], P('grp'), may hold values from 0.02 to 2
Outputs:
- update: bfloat16 [4608, 512], P('grp', 'dp')
The draws below stay inside these ranges and needn't reach their ends.
All inputs are finite; a program needn't handle non-finite values.
Results may differ from the reference program's by a relative error of at most 0.015.
Values may be sent and summed in bfloat16 or wider, within the bound.
No kernel may reach another device: no remote copies, remote signals or barrier semaphores. Data moves between devices by JAX's collectives and lax.ppermute only.
A program may use at most 64 MiB of HBM per device.

```python
import math
import jax
import jax.numpy as jnp
from jax import lax

CH = 512
HW = 14
IMG_DEV = 2
KDIM = 4608
GROUPS = 4
REPLICAS = 8
IMAGES = 64
ROWS = 12544
N_DP = 8
N_GRP = 4


def draw_out_grads(key, part):
    first = jax.random.fold_in(key, 0)
    fourth = jax.random.fold_in(key, 3)
    channel_scale = jnp.exp(jax.random.uniform(first, (CH,), jnp.float32, 0.0, math.log(10.0)))
    image_index = jnp.arange(IMAGES, dtype=jnp.int32)
    device = image_index // IMG_DEV
    replica = (device // GROUPS).astype(jnp.float32)
    member = (device % GROUPS).astype(jnp.float32)
    rise = 3.0 ** (replica / max(REPLICAS - 1, 1)) * 3.0 ** (member / max(GROUPS - 1, 1))
    base = jax.random.normal(fourth, (IMAGES, HW, HW, CH), jnp.float32)
    base = jnp.clip(base, -4.0, 4.0)
    values = 0.1 * base * channel_scale[None, None, None, :] * rise[:, None, None, None]
    return values.astype(jnp.bfloat16)


def block_scale(stream_key, extent, cuts, least, top_value):
    gain = 1.0
    for axis_at, blocks in cuts:
        draws = jax.random.uniform(jax.random.fold_in(jax.random.fold_in(stream_key, 6), axis_at), (blocks,), jnp.float32, least / len(cuts), top_value / len(cuts))
        gain = gain * jnp.repeat(jnp.exp(draws), extent[axis_at] // blocks).reshape((-1,) + (1,) * (len(extent) - 1 - axis_at))
    return gain


def noise(own_key, shape, deviation, bound, shards=(), held_as=jnp.bfloat16):
    loudness = block_scale(own_key, shape, shards, -0.22, 0.18) if shards else 1.0
    entries = jax.random.normal(own_key, shape, jnp.float32) * deviation * loudness
    return jnp.minimum(jnp.maximum(entries, -bound), bound).astype(held_as)


def setup_inputs(seed: int = 0) -> dict:
    keys = jax.random.split(jax.random.key(seed), 6)
    activations = noise(keys[0], (IMAGES, HW, HW, CH), 1.0, 6.0, ((0, 32),))
    out_grads = draw_out_grads(jax.random.fold_in(keys[5], 71), 0)
    input_basis = noise(keys[2], (KDIM, KDIM), KDIM ** -0.5, 0.09375, ((0, 4),))
    output_basis = noise(keys[3], (CH, CH), CH ** -0.5, 0.25)
    input_eigen = jnp.clip(jnp.exp(math.log(2.0) - 4.6051702 * jax.random.uniform(keys[4], (KDIM,), jnp.float32) ** block_scale(keys[4], (KDIM,), ((0, 4),), -0.2, 0.2)), 0.02, 2.0)
    return {"activations": activations, "out_grads": out_grads, "input_basis": input_basis, "output_basis": output_basis, "input_eigen": input_eigen}


damping = 1.0


def unfold(images):
    side = images.shape[1]
    channels = images.shape[3]
    padded = jnp.pad(images, ((0, 0), (1, 1), (1, 1), (0, 0)))
    pieces = [padded[:, row:row + side, col:col + side, :] for row in range(3) for col in range(3)]
    return jnp.concatenate(pieces, axis=-1).reshape(-1, 9 * channels)


def rounded(value):
    return lax.optimization_barrier(value.astype(jnp.bfloat16)).astype(jnp.float32)


def reference(activations, out_grads, input_basis, output_basis, input_eigen):
    kdim = 9 * CH
    per_group = IMG_DEV * N_GRP
    acts = activations.reshape(N_DP, per_group, HW, HW, CH)
    grads = out_grads.reshape(N_DP, per_group, HW, HW, CH)
    out_basis = output_basis.astype(jnp.float32)
    highest = lax.Precision.HIGHEST

    def one_replica(carry, pair):
        total, moment = carry
        act_block, grad_block = pair
        for member in range(N_GRP):
            images = act_block[member * IMG_DEV:(member + 1) * IMG_DEV]
            flat = grad_block[member * IMG_DEV:(member + 1) * IMG_DEV].reshape(-1, CH).astype(jnp.float32)
            turned = jnp.dot(flat, out_basis, precision=highest)
            turned_b = turned.astype(jnp.bfloat16).astype(jnp.float32)
            moment = moment + rounded(jnp.sum(turned * turned, axis=0))
            patches = unfold(images).astype(jnp.float32)
            term = jnp.dot(patches.T, turned_b, precision=highest)
            total = total + rounded(term)
        return (total, moment), None

    start = (jnp.zeros((kdim, CH), jnp.float32), jnp.zeros((CH,), jnp.float32))
    (grad_total, moment_total), _ = lax.scan(one_replica, start, (acts, grads))
    grad_mean = (grad_total / IMAGES).astype(jnp.bfloat16).astype(jnp.float32)
    eigen_out = moment_total / ROWS
    own_rows = kdim // N_GRP
    rotated = jnp.zeros((kdim, CH), jnp.float32)
    for member in range(N_GRP):
        basis_block = input_basis[member * own_rows:(member + 1) * own_rows].astype(jnp.float32)
        part = jnp.dot(basis_block.T, grad_mean[member * own_rows:(member + 1) * own_rows], precision=highest)
        rotated = rotated + rounded(part)
    scaled = (rotated / (input_eigen[:, None] * eigen_out[None, :] + damping)).astype(jnp.bfloat16)
    back = jnp.dot(input_basis.astype(jnp.float32), scaled.astype(jnp.float32), precision=highest)
    back = back.astype(jnp.bfloat16).astype(jnp.float32)
    update = jnp.dot(back, out_basis.T, precision=highest)
    return update.astype(jnp.bfloat16)
```

```python
import functools

import jax
import jax.numpy as jnp
from jax import lax
from jax.experimental import pallas as pl
from jax.experimental.pallas import tpu as pltpu
from jax.sharding import PartitionSpec as P

damping = 1.0
BF = jnp.bfloat16
F32 = jnp.float32


def unfold(images):
    side = images.shape[1]
    channels = images.shape[3]
    padded = jnp.pad(images, ((0, 0), (1, 1), (1, 1), (0, 0)))
    pieces = [
        padded[:, row : row + side, col : col + side, :] for row in range(3) for col in range(3)
    ]
    return jnp.concatenate(pieces, axis=-1).reshape(-1, 9 * channels)


def rounded(value):
    return lax.optimization_barrier(value.astype(jnp.bfloat16)).astype(jnp.float32)


def any_mesh(activations, out_grads, input_basis, output_basis, input_eigen):
    channels = output_basis.shape[0]
    side = activations.shape[1]
    local_images = activations.shape[0]
    replicas = lax.axis_size("dp")
    groups = lax.axis_size("grp")
    images_all = local_images * replicas * groups
    contract_rows = (((0,), (0,)), ((), ()))
    flat = out_grads.reshape(-1, channels)
    turned = jnp.dot(flat, output_basis, preferred_element_type=jnp.float32)
    turned_b = turned.astype(jnp.bfloat16)
    moment = rounded(jnp.sum(turned * turned, axis=0))
    patches = unfold(activations)
    term = lax.dot_general(patches, turned_b, contract_rows, preferred_element_type=jnp.float32)
    tiled = jnp.broadcast_to(moment[None, :], (groups, channels))
    group_sum, group_moment = (
        lax.psum_scatter(term.astype(jnp.bfloat16), "grp", scatter_dimension=0, tiled=True).astype(
            jnp.float32
        ),
        lax.psum_scatter(tiled.astype(jnp.bfloat16), "grp", scatter_dimension=0, tiled=True).astype(
            jnp.float32
        ),
    )
    grad_total, moment_rows = lax.psum((group_sum, group_moment), "dp")
    moment_total = moment_rows[0]
    grad_mean = (grad_total / images_all).astype(jnp.bfloat16)
    eigen_out = moment_total / (images_all * side * side)
    width = channels // replicas
    offset = lax.axis_index("dp") * width
    columns = lax.dynamic_slice_in_dim(grad_mean, offset, width, 1)
    rotated = lax.psum_scatter(
        lax.dot_general(
            input_basis, columns, contract_rows, preferred_element_type=jnp.float32
        ).astype(jnp.bfloat16),
        "grp",
        scatter_dimension=0,
        tiled=True,
    ).astype(jnp.float32)
    eigen_cols = lax.dynamic_slice_in_dim(eigen_out, offset, width, 0)
    scaled = (rotated / (input_eigen[:, None] * eigen_cols[None, :] + damping)).astype(jnp.bfloat16)
    back = jnp.dot(
        input_basis,
        lax.all_gather(scaled, "grp", axis=0, tiled=True),
        preferred_element_type=jnp.float32,
    )
    block = back.astype(jnp.bfloat16)
    out_rows = lax.dynamic_slice_in_dim(output_basis, offset, width, 0)
    final = lax.dot_general(
        lax.all_gather(block, "dp", axis=1, tiled=True),
        out_rows,
        (((1,), (1,)), ((), ())),
        preferred_element_type=jnp.float32,
    )
    return final.astype(jnp.bfloat16)


def swap(value, bit):
    return lax.ppermute(value, "dp", [(i, i ^ bit) for i in range(lax.axis_size("dp"))])


def shift(value, step):
    n = lax.axis_size("grp")
    return lax.ppermute(value, "grp", [(i, (i + step) % n) for i in range(n)])


def grad_kernel(act_a, act_b, dout_a, dout_b, basis_t, s_a, k_a, s_b, k_b, acts, turned, lhs):
    step = pl.program_id(0)
    rows = act_a.shape[0]

    @pl.when(step == 0)
    def _():
        me = lax.axis_index("dp")
        half = basis_t.shape[0] // 2
        sub = half // 8
        quarter = me >> 1
        base = (me & 1) * half
        order = [(0, 1), (0, 3), (0, 0), (0, 2), (1, 2), (1, 3), (1, 0), (1, 1)]
        for at, (chunk, flip) in enumerate(order):
            start = pl.multiple_of(base + (quarter ^ flip) * 2 * sub + chunk * sub, sub)
            turned[at * sub : (at + 1) * sub, :] = basis_t[pl.ds(start, sub), :]
        acts[0:16, :] = jnp.zeros((16, acts.shape[1]), BF)
        acts[16 + 2 * rows :, :] = jnp.zeros((16, acts.shape[1]), BF)
        acts[16 : 16 + rows, :] = act_a[...]
        acts[16 + rows : 16 + 2 * rows, :] = act_b[...]
        own = turned[...]
        for at, ref in enumerate((dout_a, dout_b)):
            part = lax.dot_general(
                own, ref[...], (((1,), (1,)), ((), ())), preferred_element_type=F32
            )
            for tap, turn in enumerate((rows - 1, 0, 1)):
                moved = pltpu.roll(part, turn, 1) if turn else part
                lhs[tap * half : (tap + 1) * half, at * rows : (at + 1) * rows] = moved.astype(BF)

    window = acts[pl.ds(pl.multiple_of(16 * step, 16), 2 * rows), :]
    out = jnp.dot(lhs[...], window, preferred_element_type=F32)
    channels = window.shape[1]
    quarter_rows = s_a.shape[0]
    for tap in range(3):
        for at, ref in enumerate((s_a, k_a, s_b, k_b)):
            start = tap * 4 * quarter_rows + at * quarter_rows
            ref[:, tap * channels : (tap + 1) * channels] = out[
                start : start + quarter_rows, :
            ].astype(BF)


def grad_parts(act_a, act_b, dout_a, dout_b, basis_t):
    rows, channels = act_a.shape
    sub = channels // 8
    whole = lambda shape: pl.BlockSpec(shape, lambda i: (0,) * len(shape))
    piece = jax.ShapeDtypeStruct((sub, 9 * channels), BF)
    return pl.pallas_call(
        grad_kernel,
        grid=(3,),
        in_specs=[whole((rows, channels))] * 4 + [whole(basis_t.shape)],
        out_specs=[pl.BlockSpec((sub, 3 * channels), lambda i: (0, i))] * 4,
        out_shape=[piece] * 4,
        scratch_shapes=[
            pltpu.VMEM((2 * rows + 32, channels), BF),
            pltpu.VMEM((channels // 2, channels), BF),
            pltpu.VMEM((3 * channels // 2, 2 * rows), BF),
        ],
        compiler_params=pltpu.CompilerParams(
            dimension_semantics=("arbitrary",), vmem_limit_bytes=40 << 20
        ),
        cost_estimate=pl.CostEstimate(
            flops=2 * 9 * channels * channels * rows,
            bytes_accessed=4 * rows * channels * 2 + 9 * channels * channels,
            transcendentals=0,
        ),
    )(act_a, act_b, dout_a, dout_b, basis_t)


def padded_rows(images):
    n, h, w, c = images.shape
    return jnp.pad(images, ((0, 0), (0, 16 - h), (0, 16 - w), (0, 0))).reshape(n * 256, c)


def spread(value, width):
    n = lax.axis_size("grp")
    me = lax.axis_index("grp")
    total = lax.dynamic_slice_in_dim(value, me * width, width, 1).astype(F32)
    for step in range(1, n):
        piece = lax.dynamic_slice_in_dim(value, lax.rem(me + step, n) * width, width, 1)
        total = total + shift(piece.astype(BF), step).astype(F32)
    return total


def cube(activations, out_grads, input_basis, output_basis, input_eigen):
    channels = output_basis.shape[0]
    local_images, side = activations.shape[:2]
    images_all = local_images * lax.axis_size("dp") * lax.axis_size("grp")
    groups = lax.axis_size("grp")
    me = lax.axis_index("dp")
    width = channels // 8
    own_rows = input_eigen.shape[0]
    block = (me & 1) * 4 + (me >> 1)

    flat = out_grads.reshape(-1, channels)
    turned = jnp.dot(flat, output_basis, preferred_element_type=F32)
    moment = rounded(jnp.sum(turned * turned, axis=0))
    for bit in (1, 2, 4):
        moment = moment + swap(moment, bit)
    parts = [moment] + [shift(moment, step) for step in range(1, groups)]
    eigen_out = sum(parts) / (images_all * side * side)
    eigen_cols = lax.dynamic_slice_in_dim(eigen_out, block * width, width, 0)

    acts = padded_rows(activations)
    douts = padded_rows(out_grads)
    s_a, k_a, s_b, k_b = grad_parts(acts, swap(acts, 1), douts, swap(douts, 1), output_basis.T)
    half = width // 2
    r_a, r_b = swap(s_a, 2), swap(s_b, 4)
    sum_a, sum_b = k_a.astype(F32) + r_a.astype(F32), k_b.astype(F32) + r_b.astype(F32)
    r_a = swap(sum_a[half:].astype(BF), 4)
    r_b = swap(sum_b[half:].astype(BF), 2)
    total = jnp.concatenate([sum_a[:half] + r_a.astype(F32), sum_b[:half] + r_b.astype(F32)], 0)
    grad_mean = (spread(total, own_rows) / images_all).astype(BF)

    rotated = spread(jnp.dot(grad_mean, input_basis, preferred_element_type=F32).astype(BF), own_rows)
    scaled = (rotated / (input_eigen[None, :] * eigen_cols[:, None] + damping)).astype(BF)

    near = jnp.concatenate([scaled] + [swap(scaled, bit) for bit in (2, 4, 6)], 0)
    pieces = [
        lax.dynamic_slice_in_dim(output_basis, (block ^ flip) * width, width, 1)
        for flip in range(4)
    ]
    mine = jnp.concatenate(pieces, 1)
    rows_of = lambda r: lax.dynamic_slice_in_dim(mine, r * width, width, 0)
    both = jnp.concatenate([rows_of(me), rows_of(me ^ 1)], 0)
    turned_back = jnp.dot(both, near, preferred_element_type=F32)
    own = (turned_back[:width] + swap(turned_back[width:], 1)).astype(BF)

    grp = lax.axis_index("grp")
    update = None
    for step in range(groups):
        held = own if step == 0 else shift(own, step)
        at = lax.rem(grp - step + groups, groups) * own_rows
        basis = lax.dynamic_slice_in_dim(input_basis, at, own_rows, 1)
        part = lax.dot_general(held, basis, (((1,), (1,)), ((), ())), preferred_element_type=F32)
        update = part if update is None else update + part
    return update.astype(BF).T


def solution(mesh):
    in_specs = (
        P(("dp", "grp"), None, None, None),
        P(("dp", "grp"), None, None, None),
        P("grp", None),
        P(),
        P("grp"),
    )
    out_specs = P("grp", "dp")
    plan = cube if mesh.shape["dp"] == 8 else any_mesh
    return jax.shard_map(plan, mesh=mesh, in_specs=in_specs, out_specs=out_specs, check_vma=False)
```

```python
import functools

import jax
import jax.numpy as jnp
from jax import lax
from jax.experimental import pallas as pl
from jax.experimental.pallas import tpu as pltpu
from jax.sharding import PartitionSpec as P

damping = 1.0
BF = jnp.bfloat16
F32 = jnp.float32
LOADS = 4


def unfold(images):
    side = images.shape[1]
    channels = images.shape[3]
    padded = jnp.pad(images, ((0, 0), (1, 1), (1, 1), (0, 0)))
    pieces = [
        padded[:, row : row + side, col : col + side, :] for row in range(3) for col in range(3)
    ]
    return jnp.concatenate(pieces, axis=-1).reshape(-1, 9 * channels)


def rounded(value):
    return lax.optimization_barrier(value.astype(jnp.bfloat16)).astype(jnp.float32)


def any_mesh(activations, out_grads, input_basis, output_basis, input_eigen):
    channels = output_basis.shape[0]
    side = activations.shape[1]
    local_images = activations.shape[0]
    replicas = lax.axis_size("dp")
    groups = lax.axis_size("grp")
    images_all = local_images * replicas * groups
    contract_rows = (((0,), (0,)), ((), ()))
    flat = out_grads.reshape(-1, channels)
    turned = jnp.dot(flat, output_basis, preferred_element_type=jnp.float32)
    turned_b = turned.astype(jnp.bfloat16)
    moment = rounded(jnp.sum(turned * turned, axis=0))
    patches = unfold(activations)
    term = lax.dot_general(patches, turned_b, contract_rows, preferred_element_type=jnp.float32)
    tiled = jnp.broadcast_to(moment[None, :], (groups, channels))
    group_sum, group_moment = (
        lax.psum_scatter(term.astype(jnp.bfloat16), "grp", scatter_dimension=0, tiled=True).astype(
            jnp.float32
        ),
        lax.psum_scatter(tiled.astype(jnp.bfloat16), "grp", scatter_dimension=0, tiled=True).astype(
            jnp.float32
        ),
    )
    grad_total, moment_rows = lax.psum((group_sum, group_moment), "dp")
    moment_total = moment_rows[0]
    grad_mean = (grad_total / images_all).astype(jnp.bfloat16)
    eigen_out = moment_total / (images_all * side * side)
    width = channels // replicas
    offset = lax.axis_index("dp") * width
    columns = lax.dynamic_slice_in_dim(grad_mean, offset, width, 1)
    rotated = lax.psum_scatter(
        lax.dot_general(
            input_basis, columns, contract_rows, preferred_element_type=jnp.float32
        ).astype(jnp.bfloat16),
        "grp",
        scatter_dimension=0,
        tiled=True,
    ).astype(jnp.float32)
    eigen_cols = lax.dynamic_slice_in_dim(eigen_out, offset, width, 0)
    scaled = (rotated / (input_eigen[:, None] * eigen_cols[None, :] + damping)).astype(jnp.bfloat16)
    back = jnp.dot(
        input_basis,
        lax.all_gather(scaled, "grp", axis=0, tiled=True),
        preferred_element_type=jnp.float32,
    )
    block = back.astype(jnp.bfloat16)
    out_rows = lax.dynamic_slice_in_dim(output_basis, offset, width, 0)
    final = lax.dot_general(
        lax.all_gather(block, "dp", axis=1, tiled=True),
        out_rows,
        (((1,), (1,)), ((), ())),
        preferred_element_type=jnp.float32,
    )
    return final.astype(jnp.bfloat16)


def swap(value, bit):
    return lax.ppermute(value, "dp", [(i, i ^ bit) for i in range(lax.axis_size("dp"))])


def shift(value, step):
    n = lax.axis_size("grp")
    return lax.ppermute(value, "grp", [(i, (i + step) % n) for i in range(n)])


ORDER = ((0, 1), (0, 3), (0, 0), (0, 2), (1, 2), (1, 3), (1, 0), (1, 1))


def grad_kernel(
    act, dout, turn, s_a, k_a, s_b, k_b, moment, acts, flipped, turned, lhs
):
    step = pl.program_id(0)
    rows = act.shape[0]
    edge = rows // 16
    images = edge // 16

    @pl.when(step == 0)
    def _():
        me = lax.axis_index("dp")
        half = turn.shape[0] // 2
        sub = half // 8
        quarter = me >> 1
        flipped[...] = turn[:, pl.ds(pl.multiple_of((me & 1) * half, half), half)].T
        for at, (chunk, flip) in enumerate(ORDER):
            start = pl.multiple_of((quarter ^ flip) * 2 * sub + chunk * sub, sub)
            turned[at * sub : (at + 1) * sub, :] = flipped[pl.ds(start, sub), :]
        acts[0:edge, :] = jnp.zeros((edge, acts.shape[1]), BF)
        acts[edge + rows :, :] = jnp.zeros((edge, acts.shape[1]), BF)
        acts[edge : edge + rows, :] = act[...]
        part = lax.dot_general(
            turned[...], dout[...], (((1,), (1,)), ((), ())), preferred_element_type=F32
        )
        moment[...] = lax.dot_general(
            jnp.ones((8, rows), F32),
            part * part,
            (((1,), (1,)), ((), ())),
            precision=lax.Precision.HIGHEST,
            preferred_element_type=F32,
        )
        for tap, by in enumerate((rows - images, 0, images)):
            moved = pltpu.roll(part, by, 1) if by else part
            lhs[tap * half : (tap + 1) * half, :] = moved.astype(BF)

    window = acts[pl.ds(pl.multiple_of(edge * step, edge), rows), :]
    out = jnp.dot(lhs[...], window, preferred_element_type=F32)
    channels = window.shape[1]
    quarter_rows = s_a.shape[0]
    for tap in range(3):
        for at, ref in enumerate((s_a, k_a, s_b, k_b)):
            start = tap * 4 * quarter_rows + at * quarter_rows
            ref[:, tap * channels : (tap + 1) * channels] = out[
                start : start + quarter_rows, :
            ].astype(BF)


def grad_parts(act, dout, turn):
    rows, channels = act.shape
    sub = channels // 8
    whole = lambda shape: pl.BlockSpec(shape, lambda i: (0,) * len(shape))
    piece = jax.ShapeDtypeStruct((sub, 9 * channels), BF)
    return pl.pallas_call(
        grad_kernel,
        grid=(3,),
        in_specs=[whole((rows, channels))] * 2
        + [whole(turn.shape)],
        out_specs=[pl.BlockSpec((sub, 3 * channels), lambda i: (0, i))] * 4
        + [whole((8, channels // 2))],
        out_shape=[piece] * 4 + [jax.ShapeDtypeStruct((8, channels // 2), F32)],
        scratch_shapes=[
            pltpu.VMEM((rows + rows // 8, channels), BF),
            pltpu.VMEM((channels // 2, channels), BF),
            pltpu.VMEM((channels // 2, channels), BF),
            pltpu.VMEM((3 * channels // 2, rows), BF),
        ],
        compiler_params=pltpu.CompilerParams(
            dimension_semantics=("arbitrary",), vmem_limit_bytes=24 << 20
        ),
        cost_estimate=pl.CostEstimate(
            flops=9 * channels * channels * rows,
            bytes_accessed=2 * rows * channels * 2 + 9 * channels * channels,
            transcendentals=0,
        ),
    )(act, dout, turn)


def map_rows(own, other):
    both = jnp.concatenate([own, other], 2)
    h, w, n, c = both.shape
    return jnp.pad(both, ((0, 16 - h), (0, 16 - w), (0, 0), (0, 0))).reshape(256 * n, c)


def load_kernel(source, target, sems):
    rows = source.shape[0] // LOADS
    copies = [
        pltpu.make_async_copy(
            source.at[pl.ds(at * rows, rows)], target.at[pl.ds(at * rows, rows)], sems.at[at]
        )
        for at in range(LOADS)
    ]
    for copy in copies:
        copy.start()
    for copy in copies:
        copy.wait()


def load(value):
    return pl.pallas_call(
        load_kernel,
        in_specs=[pl.BlockSpec(memory_space=pl.ANY)],
        out_specs=pl.BlockSpec(memory_space=pl.ANY),
        out_shape=pltpu.VMEM(value.shape, value.dtype),
        scratch_shapes=[pltpu.SemaphoreType.DMA((LOADS,))],
        compiler_params=pltpu.CompilerParams(vmem_limit_bytes=44 << 20),
        cost_estimate=pl.CostEstimate(flops=0, bytes_accessed=4 * value.size, transcendentals=0),
    )(value)


def rotate_kernel(columns, basis, out):
    out[...] = jnp.dot(columns[...], basis[...], preferred_element_type=F32).astype(BF)


def restore_kernel(columns, basis, out):
    turned = jnp.dot(basis[...], columns[...].T, preferred_element_type=F32)
    out[...] = turned.T.astype(BF)


def with_basis(kernel, columns, basis, width):
    held = pl.BlockSpec(memory_space=pltpu.VMEM)
    return pl.pallas_call(
        kernel,
        in_specs=[held, held],
        out_specs=held,
        out_shape=jax.ShapeDtypeStruct((columns.shape[0], width), BF),
        compiler_params=pltpu.CompilerParams(vmem_limit_bytes=8 << 20),
        cost_estimate=pl.CostEstimate(
            flops=2 * columns.shape[0] * basis.size, bytes_accessed=2 * basis.size, transcendentals=0
        ),
    )(columns, basis)


def spread(value, width):
    n = lax.axis_size("grp")
    me = lax.axis_index("grp")
    total = lax.dynamic_slice_in_dim(value, me * width, width, 1).astype(F32)
    for step in range(1, n):
        piece = lax.dynamic_slice_in_dim(value, lax.rem(me + step, n) * width, width, 1)
        total = total + shift(piece.astype(BF), step).astype(F32)
    return total


def cube(activations, out_grads, input_basis, output_basis, input_eigen):
    channels = output_basis.shape[0]
    local_images, side = activations.shape[:2]
    images_all = local_images * lax.axis_size("dp") * lax.axis_size("grp")
    groups = lax.axis_size("grp")
    me = lax.axis_index("dp")
    width = channels // 8
    own_rows = input_eigen.shape[0]
    block = (me & 1) * 4 + (me >> 1)

    act_own = activations.transpose(1, 2, 0, 3)
    dout_own = out_grads.transpose(1, 2, 0, 3)
    act_rows = map_rows(act_own, swap(act_own, 1))
    dout_rows = map_rows(dout_own, swap(dout_own, 1))
    s_a, k_a, s_b, k_b, moment = grad_parts(act_rows, dout_rows, output_basis)

    half = width // 2
    r_a, r_b = swap(s_a, 2), swap(s_b, 4)
    r_a, r_b, moment = lax.optimization_barrier((r_a, r_b, moment))
    sum_a, sum_b = k_a.astype(F32) + r_a.astype(F32), k_b.astype(F32) + r_b.astype(F32)
    r_a = swap(sum_a[half:].astype(BF), 4)
    r_b = swap(sum_b[half:].astype(BF), 2)
    total = jnp.concatenate([sum_a[:half] + r_a.astype(F32), sum_b[:half] + r_b.astype(F32)], 0)
    source, total = lax.optimization_barrier((input_basis, total))
    grad_mean = (spread(total, own_rows) / images_all).astype(BF)
    basis = load(source)
    rotated = spread(with_basis(rotate_kernel, grad_mean, basis, basis.shape[1]), own_rows)

    def of(terms, flip):
        places = [ORDER.index((chunk, flip)) * half for chunk in (0, 1)]
        return jnp.concatenate([terms[0:1, at : at + half] for at in places], 1)

    own_moment = of(moment, 0)
    for flip in (1, 2, 3):
        own_moment = own_moment + of(swap(moment, 2 * flip), flip)
    own_moment = sum([shift(own_moment, step) for step in range(1, groups)], own_moment)
    eigen_cols = own_moment[0] / (images_all * side * side)
    scaled = (rotated / (input_eigen[None, :] * eigen_cols[:, None] + damping)).astype(BF)

    near = jnp.concatenate([scaled] + [swap(scaled, bit) for bit in (2, 4, 6)], 0)
    pieces = [
        lax.dynamic_slice_in_dim(output_basis, (block ^ flip) * width, width, 1)
        for flip in range(4)
    ]
    mine = jnp.concatenate(pieces, 1)
    rows_of = lambda r: lax.dynamic_slice_in_dim(mine, r * width, width, 0)
    both = jnp.concatenate([rows_of(me), rows_of(me ^ 1)], 0)
    turned_back = jnp.dot(both, near, preferred_element_type=F32)
    own = (turned_back[:width] + swap(turned_back[width:], 1)).astype(BF)

    grp = lax.axis_index("grp")
    source, own = lax.optimization_barrier((input_basis, own))
    back = jnp.zeros((width, groups * own_rows), BF)
    for step in range(groups):
        block_of = own if step == 0 else shift(own, step)
        at = lax.rem(grp - step + groups, groups) * own_rows
        back = lax.dynamic_update_slice_in_dim(back, block_of, at, 1)
    basis = load(source)
    return with_basis(restore_kernel, back, basis, own_rows).T


def solution(mesh):
    in_specs = (
        P(("dp", "grp"), None, None, None),
        P(("dp", "grp"), None, None, None),
        P("grp", None),
        P(),
        P("grp"),
    )
    out_specs = P("grp", "dp")
    plan = cube if mesh.shape["dp"] == 8 else any_mesh
    return jax.shard_map(plan, mesh=mesh, in_specs=in_specs, out_specs=out_specs, check_vma=False)
```

```python
import functools

import jax
import jax.numpy as jnp
from jax import lax
from jax.experimental import pallas as pl
from jax.experimental.pallas import tpu as pltpu
from jax.sharding import PartitionSpec as P

damping = 1.0
BF = jnp.bfloat16
F32 = jnp.float32
LOADS = 8


def unfold(images):
    side = images.shape[1]
    channels = images.shape[3]
    padded = jnp.pad(images, ((0, 0), (1, 1), (1, 1), (0, 0)))
    pieces = [
        padded[:, row : row + side, col : col + side, :] for row in range(3) for col in range(3)
    ]
    return jnp.concatenate(pieces, axis=-1).reshape(-1, 9 * channels)


def rounded(value):
    return lax.optimization_barrier(value.astype(jnp.bfloat16)).astype(jnp.float32)


def any_mesh(activations, out_grads, input_basis, output_basis, input_eigen):
    channels = output_basis.shape[0]
    side = activations.shape[1]
    local_images = activations.shape[0]
    replicas = lax.axis_size("dp")
    groups = lax.axis_size("grp")
    images_all = local_images * replicas * groups
    contract_rows = (((0,), (0,)), ((), ()))
    flat = out_grads.reshape(-1, channels)
    turned = jnp.dot(flat, output_basis, preferred_element_type=jnp.float32)
    turned_b = turned.astype(jnp.bfloat16)
    moment = rounded(jnp.sum(turned * turned, axis=0))
    patches = unfold(activations)
    term = lax.dot_general(patches, turned_b, contract_rows, preferred_element_type=jnp.float32)
    tiled = jnp.broadcast_to(moment[None, :], (groups, channels))
    group_sum, group_moment = (
        lax.psum_scatter(term.astype(jnp.bfloat16), "grp", scatter_dimension=0, tiled=True).astype(
            jnp.float32
        ),
        lax.psum_scatter(tiled.astype(jnp.bfloat16), "grp", scatter_dimension=0, tiled=True).astype(
            jnp.float32
        ),
    )
    grad_total, moment_rows = lax.psum((group_sum, group_moment), "dp")
    moment_total = moment_rows[0]
    grad_mean = (grad_total / images_all).astype(jnp.bfloat16)
    eigen_out = moment_total / (images_all * side * side)
    width = channels // replicas
    offset = lax.axis_index("dp") * width
    columns = lax.dynamic_slice_in_dim(grad_mean, offset, width, 1)
    rotated = lax.psum_scatter(
        lax.dot_general(
            input_basis, columns, contract_rows, preferred_element_type=jnp.float32
        ).astype(jnp.bfloat16),
        "grp",
        scatter_dimension=0,
        tiled=True,
    ).astype(jnp.float32)
    eigen_cols = lax.dynamic_slice_in_dim(eigen_out, offset, width, 0)
    scaled = (rotated / (input_eigen[:, None] * eigen_cols[None, :] + damping)).astype(jnp.bfloat16)
    back = jnp.dot(
        input_basis,
        lax.all_gather(scaled, "grp", axis=0, tiled=True),
        preferred_element_type=jnp.float32,
    )
    block = back.astype(jnp.bfloat16)
    out_rows = lax.dynamic_slice_in_dim(output_basis, offset, width, 0)
    final = lax.dot_general(
        lax.all_gather(block, "dp", axis=1, tiled=True),
        out_rows,
        (((1,), (1,)), ((), ())),
        preferred_element_type=jnp.float32,
    )
    return final.astype(jnp.bfloat16)


def swap(value, bit):
    return lax.ppermute(value, "dp", [(i, i ^ bit) for i in range(lax.axis_size("dp"))])


def shift(value, step):
    n = lax.axis_size("grp")
    return lax.ppermute(value, "grp", [(i, (i + step) % n) for i in range(n)])


ROUTES = (((1, 3), (0, 2)), ((2, 3), (0, 1)))
ORDER = tuple(
    (2 * chunk + route, flip)
    for chunk in (0, 1)
    for route in (0, 1)
    for flips in ROUTES[route]
    for flip in flips
)


def grad_kernel(act_a, act_b, dout_a, dout_b, turn, *refs):
    pieces, (acts, flipped, turned, lhs) = refs[:8], refs[8:]
    rows, channels = act_a.shape
    edge = rows // 16
    images = edge // 16
    half = channels // 2
    sub = half // len(ORDER)
    me = lax.axis_index("dp")
    quarter = me >> 1
    flipped[...] = turn[:, pl.ds(pl.multiple_of((me & 1) * half, half), half)].T
    for at, (part, flip) in enumerate(ORDER):
        start = pl.multiple_of((quarter ^ flip) * 4 * sub + part * sub, sub)
        turned[at * sub : (at + 1) * sub, :] = flipped[pl.ds(start, sub), :]
    acts[0:edge, :] = jnp.zeros((edge, channels), BF)
    acts[edge + 2 * rows :, :] = jnp.zeros((edge, channels), BF)
    acts[edge : edge + rows, :] = act_a[...]
    acts[edge + rows : edge + 2 * rows, :] = act_b[...]
    squares = jnp.zeros((half, 128), F32)
    for at, ref in enumerate((dout_a, dout_b)):
        part = lax.dot_general(
            turned[...], ref[...], (((1,), (1,)), ((), ())), preferred_element_type=F32
        )
        for lane in range(0, rows, 128):
            squares = squares + part[:, lane : lane + 128] * part[:, lane : lane + 128]
        for tap, by in enumerate((rows - images, 0, images)):
            moved = pltpu.roll(part, by, 1) if by else part
            lhs[tap * half : (tap + 1) * half, at * rows : (at + 1) * rows] = moved.astype(BF)
    for at, ref in enumerate(pieces):
        ref[:, 9 * channels :] = squares[at * 2 * sub : (at + 1) * 2 * sub, :].astype(BF)
    for step in range(3):
        window = acts[edge * step : edge * step + 2 * rows, :]
        out = jnp.dot(lhs[...], window, preferred_element_type=F32)
        for tap in range(3):
            column = (3 * step + tap) * channels
            for at, ref in enumerate(pieces):
                start = tap * half + at * 2 * sub
                ref[:, column : column + channels] = out[start : start + 2 * sub, :].astype(BF)


def grad_parts(act_a, act_b, dout_a, dout_b, turn):
    rows, channels = act_a.shape
    half = channels // 2
    near = pl.BlockSpec(memory_space=pltpu.VMEM)
    return pl.pallas_call(
        grad_kernel,
        in_specs=[near] * 5,
        out_specs=[near] * 8,
        out_shape=[jax.ShapeDtypeStruct((half // 8, 9 * channels + 128), BF)] * 8,
        scratch_shapes=[
            pltpu.VMEM((2 * rows + rows // 8, channels), BF),
            pltpu.VMEM((half, channels), BF),
            pltpu.VMEM((half, channels), BF),
            pltpu.VMEM((3 * half, 2 * rows), BF),
        ],
        compiler_params=pltpu.CompilerParams(vmem_limit_bytes=16 << 20),
        cost_estimate=pl.CostEstimate(
            flops=18 * channels * channels * rows,
            bytes_accessed=4 * rows * channels * 2 + 9 * channels * channels,
            transcendentals=0,
        ),
    )(act_a, act_b, dout_a, dout_b, turn)


def map_rows(images):
    h, w, n, c = images.shape
    return jnp.pad(images, ((0, 16 - h), (0, 16 - w), (0, 0), (0, 0))).reshape(256 * n, c)


def load_kernel(source, after, target, sems):
    del after
    rows = source.shape[0] // LOADS
    copies = [
        pltpu.make_async_copy(
            source.at[pl.ds(at * rows, rows)], target.at[pl.ds(at * rows, rows)], sems.at[at]
        )
        for at in range(LOADS)
    ]
    for copy in copies:
        copy.start()
    for copy in copies:
        copy.wait()


def load(value, after):
    return pl.pallas_call(
        load_kernel,
        in_specs=[pl.BlockSpec(memory_space=pl.ANY), pl.BlockSpec(memory_space=pltpu.VMEM)],
        out_specs=pl.BlockSpec(memory_space=pl.ANY),
        out_shape=pltpu.VMEM(value.shape, value.dtype),
        scratch_shapes=[pltpu.SemaphoreType.DMA((LOADS,))],
        compiler_params=pltpu.CompilerParams(vmem_limit_bytes=44 << 20),
        cost_estimate=pl.CostEstimate(flops=0, bytes_accessed=4 * value.size, transcendentals=0),
    )(value, after)


def stage(kernel, out_shape, operands, after=(), flops=0):
    near = pl.BlockSpec(memory_space=pltpu.VMEM)

    def body(*refs):
        kernel(refs[: len(operands)], refs[len(operands) + len(after) :])

    results = pl.pallas_call(
        body,
        in_specs=[near] * (len(operands) + len(after)),
        out_specs=[near] * len(out_shape),
        out_shape=out_shape,
        compiler_params=pltpu.CompilerParams(vmem_limit_bytes=8 << 20),
        cost_estimate=pl.CostEstimate(
            flops=flops, bytes_accessed=sum(2 * x.size for x in operands), transcendentals=0
        ),
    )(*operands, *after)
    return list(results)


def first_sum(ins, outs):
    kept, sent = outs[0], outs[1:]
    sub = sent[0].shape[0]
    for route in (0, 1):
        mine, came = ins[2 * route], ins[2 * route + 1]
        low, high = slice(0, sub), slice(sub, 2 * sub)
        kept[route * sub : (route + 1) * sub, :] = mine[low, :].astype(F32) + came[low, :].astype(
            F32
        )
        sent[route][...] = (mine[high, :].astype(F32) + came[high, :].astype(F32)).astype(BF)


def deal(value, outs, width, behind=None):
    me = lax.axis_index("grp")
    groups = len(outs)
    for step, out in enumerate(outs):
        at = pl.multiple_of(lax.rem(me + step, groups) * width, 128)
        out[:, 0:width] = value[:, pl.ds(at, width)].astype(out.dtype)
        if behind is not None:
            out[:, width:] = behind.astype(out.dtype)


def second_sum(ins, outs):
    kept, came_a, came_b = ins
    *outs, total = outs
    sub = came_a.shape[0]
    total[0:sub, :] = kept[0:sub, :] + came_a[...].astype(F32)
    total[sub:, :] = kept[sub:, :] + came_b[...].astype(F32)
    rows, width = outs[0].shape
    deal(total, outs, width - 128, total[:, len(outs) * (width - 128) :])


def gathered(ins):
    total = ins[0][...]
    for other in ins[1:]:
        total = total + other[...].astype(F32)
    return total


def rotate(ins, outs, images_all):
    *ins, basis = ins
    *outs, moments, product = outs
    sums = gathered(ins)
    rows = basis.shape[0]
    grad_mean = (sums[:, :rows] / images_all).astype(BF)
    moments[...] = sums[:, rows:]
    product[...] = jnp.dot(grad_mean, basis[...], preferred_element_type=F32).astype(BF)
    deal(product, outs, rows)


def rescale(ins, outs, positions):
    *ins, moments, input_eigen = ins
    eigen_out = jnp.sum(moments[...], axis=1, keepdims=True) / positions
    outs[0][...] = (gathered(ins) / (input_eigen[...] * eigen_out + damping)).astype(BF)


def restore_kernel(offset, columns, basis, held, out, *, first, last):
    width = columns.shape[1]
    block = basis[:, pl.ds(pl.multiple_of(offset[0], 128), width)]
    part = jnp.dot(block, columns[...].T, preferred_element_type=F32)
    if not first:
        part = part + held[...]
    out[...] = part.T.astype(BF) if last else part


def restore(offset, columns, basis, held, last):
    first = held is None
    rows, width = basis.shape[0], columns.shape[0]
    near = pl.BlockSpec(memory_space=pltpu.VMEM)
    kernel = functools.partial(restore_kernel, first=first, last=last)
    if first:
        held = jnp.zeros((8, 128), F32)
    return pl.pallas_call(
        kernel,
        in_specs=[pl.BlockSpec(memory_space=pltpu.SMEM), near, near, near],
        out_specs=near,
        out_shape=jax.ShapeDtypeStruct((width, rows), BF)
        if last
        else jax.ShapeDtypeStruct((rows, width), F32),
        compiler_params=pltpu.CompilerParams(vmem_limit_bytes=8 << 20),
        cost_estimate=pl.CostEstimate(
            flops=2 * columns.size * rows, bytes_accessed=2 * columns.size, transcendentals=0
        ),
    )(offset.reshape(1), columns, basis, held)


def cube(activations, out_grads, input_basis, output_basis, input_eigen):
    channels = output_basis.shape[0]
    local_images, side = activations.shape[:2]
    images_all = local_images * lax.axis_size("dp") * lax.axis_size("grp")
    groups = lax.axis_size("grp")
    me = lax.axis_index("dp")
    width = channels // 8
    own_rows = input_eigen.shape[0]
    block = (me & 1) * 4 + (me >> 1)

    act_own = activations.transpose(1, 2, 0, 3)
    dout_own = out_grads.transpose(1, 2, 0, 3)
    act_rows = [map_rows(act_own), map_rows(swap(act_own, 1))]
    dout_rows = [map_rows(dout_own), map_rows(swap(dout_own, 1))]
    parts = grad_parts(*act_rows, *dout_rows, output_basis)

    sub = width // 4
    wide = groups * own_rows + 128
    chunks = (0, 1)
    like = jax.ShapeDtypeStruct
    others = groups - 1
    came = [
        [parts[4 * c + 1], swap(parts[4 * c], 2), parts[4 * c + 3], swap(parts[4 * c + 2], 4)]
        for c in chunks
    ]
    last = ()
    for c in chunks:
        shapes = [like((2 * sub, wide), F32)] + [like((sub, wide), BF)] * 2
        kept, s_a, s_b = last = stage(first_sum, shapes, came[c], last[1:2])
        came[c] = [kept, swap(s_a, 4), swap(s_b, 2)]
    last = ()
    for c in chunks:
        shapes = [like((2 * sub, own_rows + 128), t) for t in [F32] + [BF] * others]
        last = stage(second_sum, shapes + [like((2 * sub, wide), F32)], came[c], last[1:2])
        came[c] = [last[0]] + [shift(last[step], step) for step in range(1, groups)]
        if c == 0:
            basis = load(input_basis, last[1])
    last = ()
    for c in chunks:
        shapes = [like((2 * sub, own_rows), t) for t in [F32] + [BF] * others]
        shapes += [like((2 * sub, 128), F32), like((2 * sub, groups * own_rows), BF)]
        last = stage(
            functools.partial(rotate, images_all=images_all),
            shapes,
            came[c] + [basis],
            last[1:2],
            4 * sub * input_basis.size,
        )
        came[c] = [last[0]] + [shift(last[step], step) for step in range(1, groups)]
        came[c].append(last[groups])
        if c == 0:
            basis = load(input_basis, last[1])

    both = jnp.concatenate(
        [lax.dynamic_slice_in_dim(output_basis, r * width, width, 0) for r in (me, me ^ 1)], 0
    )
    near = []
    last = ()
    for c in chunks:
        last = stage(
            functools.partial(rescale, positions=images_all * side * side),
            [like((2 * sub, own_rows), BF)],
            came[c] + [input_eigen.reshape(1, own_rows)],
            last,
        )
        near.append(last + [swap(last[0], bit) for bit in (2, 4, 6)])
    turned_back = 0
    for chunk in chunks:
        columns = [
            lax.dynamic_slice_in_dim(both, (block ^ flip) * width + 2 * sub * chunk, 2 * sub, 1)
            for flip in range(4)
        ]
        turned_back = turned_back + jnp.dot(
            jnp.concatenate(columns, 1),
            jnp.concatenate(near[chunk], 0),
            preferred_element_type=F32,
        )
    own = (turned_back[:width] + swap(turned_back[width:], 1)).astype(BF)

    grp = lax.axis_index("grp")
    basis = load(input_basis, own)
    update = None
    for step in range(groups):
        held = own if step == 0 else shift(own, step)
        at = lax.rem(grp - step + groups, groups) * own_rows
        update = restore(at, held, basis, update, step == groups - 1)
    return update.T


def solution(mesh):
    in_specs = (
        P(("dp", "grp"), None, None, None),
        P(("dp", "grp"), None, None, None),
        P("grp", None),
        P(),
        P("grp"),
    )
    out_specs = P("grp", "dp")
    plan = cube if mesh.shape["dp"] == 8 else any_mesh
    return jax.shard_map(plan, mesh=mesh, in_specs=in_specs, out_specs=out_specs, check_vma=False)
```

```python
import functools

import jax
import jax.numpy as jnp
from jax import lax
from jax.experimental import pallas as pl
from jax.experimental.pallas import tpu as pltpu
from jax.sharding import PartitionSpec as P

damping = 1.0
BF = jnp.bfloat16
F32 = jnp.float32
LOADS = 8


def unfold(images):
    side = images.shape[1]
    channels = images.shape[3]
    padded = jnp.pad(images, ((0, 0), (1, 1), (1, 1), (0, 0)))
    pieces = [
        padded[:, row : row + side, col : col + side, :] for row in range(3) for col in range(3)
    ]
    return jnp.concatenate(pieces, axis=-1).reshape(-1, 9 * channels)


def rounded(value):
    return lax.optimization_barrier(value.astype(jnp.bfloat16)).astype(jnp.float32)


def any_mesh(activations, out_grads, input_basis, output_basis, input_eigen):
    channels = output_basis.shape[0]
    side = activations.shape[1]
    local_images = activations.shape[0]
    replicas = lax.axis_size("dp")
    groups = lax.axis_size("grp")
    images_all = local_images * replicas * groups
    contract_rows = (((0,), (0,)), ((), ()))
    flat = out_grads.reshape(-1, channels)
    turned = jnp.dot(flat, output_basis, preferred_element_type=jnp.float32)
    turned_b = turned.astype(jnp.bfloat16)
    moment = rounded(jnp.sum(turned * turned, axis=0))
    patches = unfold(activations)
    term = lax.dot_general(patches, turned_b, contract_rows, preferred_element_type=jnp.float32)
    tiled = jnp.broadcast_to(moment[None, :], (groups, channels))
    group_sum, group_moment = (
        lax.psum_scatter(term.astype(jnp.bfloat16), "grp", scatter_dimension=0, tiled=True).astype(
            jnp.float32
        ),
        lax.psum_scatter(tiled.astype(jnp.bfloat16), "grp", scatter_dimension=0, tiled=True).astype(
            jnp.float32
        ),
    )
    grad_total, moment_rows = lax.psum((group_sum, group_moment), "dp")
    moment_total = moment_rows[0]
    grad_mean = (grad_total / images_all).astype(jnp.bfloat16)
    eigen_out = moment_total / (images_all * side * side)
    width = channels // replicas
    offset = lax.axis_index("dp") * width
    columns = lax.dynamic_slice_in_dim(grad_mean, offset, width, 1)
    rotated = lax.psum_scatter(
        lax.dot_general(
            input_basis, columns, contract_rows, preferred_element_type=jnp.float32
        ).astype(jnp.bfloat16),
        "grp",
        scatter_dimension=0,
        tiled=True,
    ).astype(jnp.float32)
    eigen_cols = lax.dynamic_slice_in_dim(eigen_out, offset, width, 0)
    scaled = (rotated / (input_eigen[:, None] * eigen_cols[None, :] + damping)).astype(jnp.bfloat16)
    back = jnp.dot(
        input_basis,
        lax.all_gather(scaled, "grp", axis=0, tiled=True),
        preferred_element_type=jnp.float32,
    )
    block = back.astype(jnp.bfloat16)
    out_rows = lax.dynamic_slice_in_dim(output_basis, offset, width, 0)
    final = lax.dot_general(
        lax.all_gather(block, "dp", axis=1, tiled=True),
        out_rows,
        (((1,), (1,)), ((), ())),
        preferred_element_type=jnp.float32,
    )
    return final.astype(jnp.bfloat16)


def swap(value, bit):
    return lax.ppermute(value, "dp", [(i, i ^ bit) for i in range(lax.axis_size("dp"))])


def shift(value, step):
    n = lax.axis_size("grp")
    return lax.ppermute(value, "grp", [(i, (i + step) % n) for i in range(n)])


ROUTES = (((1, 3), (0, 2)), ((2, 3), (0, 1)))
ORDER = tuple(
    (2 * chunk + route, flip)
    for chunk in (0, 1)
    for route in (0, 1)
    for flips in ROUTES[route]
    for flip in flips
)


def grad_kernel(act_a, act_b, dout_a, dout_b, turn, *refs):
    pieces, (acts, flipped, turned, lhs) = refs[:8], refs[8:]
    rows, channels = act_a.shape
    edge = rows // 16
    images = edge // 16
    half = channels // 2
    sub = half // len(ORDER)
    me = lax.axis_index("dp")
    quarter = me >> 1
    flipped[...] = turn[:, pl.ds(pl.multiple_of((me & 1) * half, half), half)].T
    for at, (part, flip) in enumerate(ORDER):
        start = pl.multiple_of((quarter ^ flip) * 4 * sub + part * sub, sub)
        turned[at * sub : (at + 1) * sub, :] = flipped[pl.ds(start, sub), :]
    acts[0:edge, :] = jnp.zeros((edge, channels), BF)
    acts[edge + 2 * rows :, :] = jnp.zeros((edge, channels), BF)
    acts[edge : edge + rows, :] = act_a[...]
    acts[edge + rows : edge + 2 * rows, :] = act_b[...]
    squares = jnp.zeros((half, 128), F32)
    for at, ref in enumerate((dout_a, dout_b)):
        part = lax.dot_general(
            turned[...], ref[...], (((1,), (1,)), ((), ())), preferred_element_type=F32
        )
        for lane in range(0, rows, 128):
            squares = squares + part[:, lane : lane + 128] * part[:, lane : lane + 128]
        for tap, by in enumerate((rows - images, 0, images)):
            moved = pltpu.roll(part, by, 1) if by else part
            lhs[tap * half : (tap + 1) * half, at * rows : (at + 1) * rows] = moved.astype(BF)
    for at, ref in enumerate(pieces):
        ref[:, 9 * channels :] = squares[at * 2 * sub : (at + 1) * 2 * sub, :].astype(BF)
    for step in range(3):
        window = acts[edge * step : edge * step + 2 * rows, :]
        out = jnp.dot(lhs[...], window, preferred_element_type=F32)
        for tap in range(3):
            column = (3 * step + tap) * channels
            for at, ref in enumerate(pieces):
                start = tap * half + at * 2 * sub
                ref[:, column : column + channels] = out[start : start + 2 * sub, :].astype(BF)


def grad_parts(act_a, act_b, dout_a, dout_b, turn):
    rows, channels = act_a.shape
    half = channels // 2
    near = pl.BlockSpec(memory_space=pltpu.VMEM)
    return pl.pallas_call(
        grad_kernel,
        in_specs=[near] * 5,
        out_specs=[near] * 8,
        out_shape=[jax.ShapeDtypeStruct((half // 8, 9 * channels + 128), BF)] * 8,
        scratch_shapes=[
            pltpu.VMEM((2 * rows + rows // 8, channels), BF),
            pltpu.VMEM((half, channels), BF),
            pltpu.VMEM((half, channels), BF),
            pltpu.VMEM((3 * half, 2 * rows), BF),
        ],
        compiler_params=pltpu.CompilerParams(vmem_limit_bytes=16 << 20),
        cost_estimate=pl.CostEstimate(
            flops=18 * channels * channels * rows,
            bytes_accessed=4 * rows * channels * 2 + 9 * channels * channels,
            transcendentals=0,
        ),
    )(act_a, act_b, dout_a, dout_b, turn)


def map_rows(images):
    h, w, n, c = images.shape
    return jnp.pad(images, ((0, 16 - h), (0, 16 - w), (0, 0), (0, 0))).reshape(256 * n, c)


def load_kernel(source, after, target, sems):
    del after
    rows = source.shape[0] // LOADS
    copies = [
        pltpu.make_async_copy(
            source.at[pl.ds(at * rows, rows)], target.at[pl.ds(at * rows, rows)], sems.at[at]
        )
        for at in range(LOADS)
    ]
    for copy in copies:
        copy.start()
    for copy in copies:
        copy.wait()


def load(value, after):
    return pl.pallas_call(
        load_kernel,
        in_specs=[pl.BlockSpec(memory_space=pl.ANY), pl.BlockSpec(memory_space=pltpu.VMEM)],
        out_specs=pl.BlockSpec(memory_space=pl.ANY),
        out_shape=pltpu.VMEM(value.shape, value.dtype),
        scratch_shapes=[pltpu.SemaphoreType.DMA((LOADS,))],
        compiler_params=pltpu.CompilerParams(vmem_limit_bytes=44 << 20),
        cost_estimate=pl.CostEstimate(flops=0, bytes_accessed=4 * value.size, transcendentals=0),
    )(value, after)


def stage(kernel, out_shape, operands, after=(), flops=0):
    near = pl.BlockSpec(memory_space=pltpu.VMEM)

    def body(*refs):
        kernel(refs[: len(operands)], refs[len(operands) + len(after) :])

    results = pl.pallas_call(
        body,
        in_specs=[near] * (len(operands) + len(after)),
        out_specs=[near] * len(out_shape),
        out_shape=out_shape,
        compiler_params=pltpu.CompilerParams(vmem_limit_bytes=8 << 20),
        cost_estimate=pl.CostEstimate(
            flops=flops, bytes_accessed=sum(2 * x.size for x in operands), transcendentals=0
        ),
    )(*operands, *after)
    return list(results)


def first_sum(ins, outs):
    kept, sent = outs[0], outs[1:]
    sub = sent[0].shape[0]
    for route in (0, 1):
        mine, came = ins[2 * route], ins[2 * route + 1]
        low, high = slice(0, sub), slice(sub, 2 * sub)
        kept[route * sub : (route + 1) * sub, :] = mine[low, :].astype(F32) + came[low, :].astype(
            F32
        )
        sent[route][...] = (mine[high, :].astype(F32) + came[high, :].astype(F32)).astype(BF)


def deal(value, outs, width, behind=None):
    me = lax.axis_index("grp")
    groups = len(outs)
    for step, out in enumerate(outs):
        at = pl.multiple_of(lax.rem(me + step, groups) * width, 128)
        out[:, 0:width] = value[:, pl.ds(at, width)].astype(out.dtype)
        if behind is not None:
            out[:, width:] = behind.astype(out.dtype)


def second_sum(ins, outs):
    *outs, total = outs
    sub = ins[1].shape[0]
    for at in (0, 1):
        kept, *others = ins[3 * at : 3 * at + 3]
        for route, came in enumerate(others):
            low = 2 * sub * at + route * sub
            total[low : low + sub, :] = kept[route * sub : (route + 1) * sub, :] + came[
                ...
            ].astype(F32)
    rows, width = outs[0].shape
    deal(total, outs, width - 128, total[:, len(outs) * (width - 128) :])


def gathered(ins):
    total = ins[0][...]
    for other in ins[1:]:
        total = total + other[...].astype(F32)
    return total


def prepare(ins, outs, images_all):
    sums = gathered(ins)
    rows = outs[0].shape[1]
    outs[0][...] = (sums[:, :rows] / images_all).astype(BF)
    outs[1][...] = sums[:, rows:]


def rotate(ins, outs, spans):
    columns, basis = ins
    me = lax.axis_index("grp")
    rows = basis.shape[0]
    groups = len(outs) // len(spans)
    for step in range(groups):
        at = pl.multiple_of(lax.rem(me + step, groups) * rows, 128)
        part = jnp.dot(columns[...], basis[:, pl.ds(at, rows)], preferred_element_type=F32)
        for c, (low, high) in enumerate(spans):
            out = outs[groups * c + step]
            out[...] = part[:, low:high].astype(BF).astype(out.dtype)


def rescale(ins, outs, positions, offset):
    *ins, moments, input_eigen = ins
    eigen_out = jnp.sum(moments[...], axis=1, keepdims=True) / positions
    chunk = outs[0].shape[1]
    scale = input_eigen[:, offset : offset + chunk] * eigen_out + damping
    outs[0][...] = (gathered(ins) / scale).astype(BF)


def turn_back(ins, outs):
    *near, weights = ins
    width = near[0].shape[0]
    total = None
    for at, block in enumerate(near):
        part = jnp.dot(
            weights[:, at * width : (at + 1) * width], block[...], preferred_element_type=F32
        )
        total = part if total is None else total + part
    outs[0][...] = total[:width]
    outs[1][...] = total[width:]


def merge(ins, outs):
    outs[0][...] = (ins[0][...] + ins[1][...]).astype(BF)


def restore(ins, outs, steps, offset, last):
    *blocks, basis = ins
    me = lax.axis_index("grp")
    rows = basis.shape[0]
    groups = basis.shape[1] // rows
    total = None
    if len(blocks) > len(steps):
        total = blocks.pop()[...]
    for step, block in zip(steps, blocks):
        chunk = block.shape[1]
        at = pl.multiple_of(lax.rem(me - step + groups, groups) * rows + offset, 128)
        part = jnp.dot(
            basis[:, pl.ds(at, chunk)], block[...].T, preferred_element_type=F32
        )
        total = part if total is None else total + part
    outs[0][...] = total.T.astype(BF) if last else total


def cube(activations, out_grads, input_basis, output_basis, input_eigen):
    channels = output_basis.shape[0]
    local_images, side = activations.shape[:2]
    images_all = local_images * lax.axis_size("dp") * lax.axis_size("grp")
    groups = lax.axis_size("grp")
    me = lax.axis_index("dp")
    width = channels // 8
    own_rows = input_eigen.shape[0]
    block = (me & 1) * 4 + (me >> 1)

    act_own = activations.transpose(1, 2, 0, 3)
    dout_own = out_grads.transpose(1, 2, 0, 3)
    act_rows = [map_rows(act_own), map_rows(swap(act_own, 1))]
    dout_rows = [map_rows(dout_own), map_rows(swap(dout_own, 1))]
    parts = grad_parts(*act_rows, *dout_rows, output_basis)

    both = jnp.concatenate(
        [lax.dynamic_slice_in_dim(output_basis, r * width, width, 0) for r in (me, me ^ 1)], 0
    )
    weights = jnp.concatenate(
        [
            lax.dynamic_slice_in_dim(both, (block ^ flip) * width, width, 1)
            for flip in range(4)
        ],
        1,
    )

    sub = width // 4
    wide = groups * own_rows + 128
    like = jax.ShapeDtypeStruct
    grp_types = [F32] + [BF] * (groups - 1)
    came = [
        [parts[4 * c + 1], swap(parts[4 * c], 2), parts[4 * c + 3], swap(parts[4 * c + 2], 4)]
        for c in (0, 1)
    ]
    basis = load(input_basis, parts[1])
    sums = ()
    for c in (0, 1):
        shapes = [like((2 * sub, wide), F32)] + [like((sub, wide), BF)] * 2
        kept, s_a, s_b = sums = stage(first_sum, shapes, came[c], sums[1:2])
        came[c] = [kept, swap(s_a, 4), swap(s_b, 2)]
    shapes = [like((width, own_rows + 128), t) for t in grp_types] + [like((width, wide), F32)]
    own, *others = stage(second_sum, shapes, came[0] + came[1])[:groups]
    came = [own] + [shift(value, step + 1) for step, value in enumerate(others)]
    columns, moments = stage(
        functools.partial(prepare, images_all=images_all),
        [like((width, own_rows), BF), like((width, 128), F32)],
        came,
    )

    spans = ((0, own_rows // 128 // 2 * 128), (own_rows // 128 // 2 * 128, own_rows))
    eigen_row = input_eigen.reshape(1, own_rows)
    rotated = stage(
        functools.partial(rotate, spans=spans),
        [like((width, high - low), t) for low, high in spans for t in grp_types],
        [columns, basis],
        (),
        2 * width * input_basis.size,
    )
    came = []
    for c in (0, 1):
        own, *others = rotated[groups * c : groups * (c + 1)]
        came.append([own] + [shift(value, step + 1) for step, value in enumerate(others)])
    near, scaled = [], ()
    for (low, high), values in zip(spans, came):
        scaled = stage(
            functools.partial(rescale, positions=images_all * side * side, offset=low),
            [like((width, high - low), BF)],
            values + [moments, eigen_row],
            scaled,
        )
        near.append(scaled + [swap(scaled[0], bit) for bit in (2, 4, 6)])
    held = []
    for (low, high), values in zip(spans, near):
        mine, sent = stage(
            turn_back,
            [like((width, high - low), F32)] * 2,
            values + [weights],
            (),
            16 * width * width * (high - low),
        )
        (own,) = stage(merge, [like((width, high - low), BF)], [mine, swap(sent, 1)])
        held.append([own] + [shift(own, step) for step in range(1, groups)])

    update = []
    calls = [(0, (0,)), (1, (0,)), (0, tuple(range(1, groups)))]
    calls += [(1, (step,)) for step in range(1, groups)]
    for at, (c, steps) in enumerate(calls):
        last = at == len(calls) - 1
        update = stage(
            functools.partial(restore, steps=steps, offset=spans[c][0], last=last),
            [like((width, own_rows), BF) if last else like((own_rows, width), F32)],
            [held[c][step] for step in steps] + update + [basis],
            (),
            2 * len(steps) * width * own_rows * held[c][0].shape[1],
        )
    return update[0].T


def solution(mesh):
    in_specs = (
        P(("dp", "grp"), None, None, None),
        P(("dp", "grp"), None, None, None),
        P("grp", None),
        P(),
        P("grp"),
    )
    out_specs = P("grp", "dp")
    plan = cube if mesh.shape["dp"] == 8 else any_mesh
    return jax.shard_map(plan, mesh=mesh, in_specs=in_specs, out_specs=out_specs, check_vma=False)
```

```python
import functools

import jax
import jax.numpy as jnp
from jax import lax
from jax.experimental import pallas as pl
from jax.experimental.pallas import tpu as pltpu
from jax.sharding import PartitionSpec as P

damping = 1.0
BF = jnp.bfloat16
F32 = jnp.float32
WORK = [[75000000, 0], [400000000, 1000000000], [75000000, 75000000], [400000000, 0], [30000000, 150000000], [400000000, 1000000000], [400000000, 400000000]]
LOADS = 8


def unfold(images):
    side = images.shape[1]
    channels = images.shape[3]
    padded = jnp.pad(images, ((0, 0), (1, 1), (1, 1), (0, 0)))
    pieces = [
        padded[:, row : row + side, col : col + side, :] for row in range(3) for col in range(3)
    ]
    return jnp.concatenate(pieces, axis=-1).reshape(-1, 9 * channels)


def rounded(value):
    return lax.optimization_barrier(value.astype(jnp.bfloat16)).astype(jnp.float32)


def any_mesh(activations, out_grads, input_basis, output_basis, input_eigen):
    channels = output_basis.shape[0]
    side = activations.shape[1]
    local_images = activations.shape[0]
    replicas = lax.axis_size("dp")
    groups = lax.axis_size("grp")
    images_all = local_images * replicas * groups
    contract_rows = (((0,), (0,)), ((), ()))
    flat = out_grads.reshape(-1, channels)
    turned = jnp.dot(flat, output_basis, preferred_element_type=jnp.float32)
    turned_b = turned.astype(jnp.bfloat16)
    moment = rounded(jnp.sum(turned * turned, axis=0))
    patches = unfold(activations)
    term = lax.dot_general(patches, turned_b, contract_rows, preferred_element_type=jnp.float32)
    tiled = jnp.broadcast_to(moment[None, :], (groups, channels))
    group_sum, group_moment = (
        lax.psum_scatter(term.astype(jnp.bfloat16), "grp", scatter_dimension=0, tiled=True).astype(
            jnp.float32
        ),
        lax.psum_scatter(tiled.astype(jnp.bfloat16), "grp", scatter_dimension=0, tiled=True).astype(
            jnp.float32
        ),
    )
    grad_total, moment_rows = lax.psum((group_sum, group_moment), "dp")
    moment_total = moment_rows[0]
    grad_mean = (grad_total / images_all).astype(jnp.bfloat16)
    eigen_out = moment_total / (images_all * side * side)
    width = channels // replicas
    offset = lax.axis_index("dp") * width
    columns = lax.dynamic_slice_in_dim(grad_mean, offset, width, 1)
    rotated = lax.psum_scatter(
        lax.dot_general(
            input_basis, columns, contract_rows, preferred_element_type=jnp.float32
        ).astype(jnp.bfloat16),
        "grp",
        scatter_dimension=0,
        tiled=True,
    ).astype(jnp.float32)
    eigen_cols = lax.dynamic_slice_in_dim(eigen_out, offset, width, 0)
    scaled = (rotated / (input_eigen[:, None] * eigen_cols[None, :] + damping)).astype(jnp.bfloat16)
    back = jnp.dot(
        input_basis,
        lax.all_gather(scaled, "grp", axis=0, tiled=True),
        preferred_element_type=jnp.float32,
    )
    block = back.astype(jnp.bfloat16)
    out_rows = lax.dynamic_slice_in_dim(output_basis, offset, width, 0)
    final = lax.dot_general(
        lax.all_gather(block, "dp", axis=1, tiled=True),
        out_rows,
        (((1,), (1,)), ((), ())),
        preferred_element_type=jnp.float32,
    )
    return final.astype(jnp.bfloat16)


def swap(value, bit):
    return lax.ppermute(value, "dp", [(i, i ^ bit) for i in range(lax.axis_size("dp"))])


def shift(value, step):
    n = lax.axis_size("grp")
    return lax.ppermute(value, "grp", [(i, (i + step) % n) for i in range(n)])


ROUTES = (((1, 3), (0, 2)), ((2, 3), (0, 1)))
ORDER = tuple(
    (2 * chunk + route, flip)
    for chunk in (0, 1)
    for route in (0, 1)
    for flips in ROUTES[route]
    for flip in flips
)


def grad_kernel(act_a, act_b, dout_a, dout_b, turn, *refs):
    pieces, (acts, flipped, turned, lhs) = refs[:8], refs[8:]
    rows, channels = act_a.shape
    edge = rows // 16
    images = edge // 16
    half = channels // 2
    sub = half // len(ORDER)
    me = lax.axis_index("dp")
    quarter = me >> 1
    flipped[...] = turn[:, pl.ds(pl.multiple_of((me & 1) * half, half), half)].T
    for at, (part, flip) in enumerate(ORDER):
        start = pl.multiple_of((quarter ^ flip) * 4 * sub + part * sub, sub)
        turned[at * sub : (at + 1) * sub, :] = flipped[pl.ds(start, sub), :]
    acts[0:edge, :] = jnp.zeros((edge, channels), BF)
    acts[edge + 2 * rows :, :] = jnp.zeros((edge, channels), BF)
    acts[edge : edge + rows, :] = act_a[...]
    acts[edge + rows : edge + 2 * rows, :] = act_b[...]
    squares = jnp.zeros((half, 128), F32)
    for at, ref in enumerate((dout_a, dout_b)):
        part = lax.dot_general(
            turned[...], ref[...], (((1,), (1,)), ((), ())), preferred_element_type=F32
        )
        for lane in range(0, rows, 128):
            squares = squares + part[:, lane : lane + 128] * part[:, lane : lane + 128]
        for tap, by in enumerate((rows - images, 0, images)):
            moved = pltpu.roll(part, by, 1) if by else part
            lhs[tap * half : (tap + 1) * half, at * rows : (at + 1) * rows] = moved.astype(BF)
    for at, ref in enumerate(pieces):
        ref[:, 9 * channels :] = squares[at * 2 * sub : (at + 1) * 2 * sub, :].astype(BF)
    for step in range(3):
        window = acts[edge * step : edge * step + 2 * rows, :]
        out = jnp.dot(lhs[...], window, preferred_element_type=F32)
        for tap in range(3):
            column = (3 * step + tap) * channels
            for at, ref in enumerate(pieces):
                start = tap * half + at * 2 * sub
                ref[:, column : column + channels] = out[start : start + 2 * sub, :].astype(BF)


def grad_parts(act_a, act_b, dout_a, dout_b, turn):
    rows, channels = act_a.shape
    half = channels // 2
    near = pl.BlockSpec(memory_space=pltpu.VMEM)
    return pl.pallas_call(
        grad_kernel,
        in_specs=[near] * 5,
        out_specs=[near] * 8,
        out_shape=[jax.ShapeDtypeStruct((half // 8, 9 * channels + 128), BF)] * 8,
        scratch_shapes=[
            pltpu.VMEM((2 * rows + rows // 8, channels), BF),
            pltpu.VMEM((half, channels), BF),
            pltpu.VMEM((half, channels), BF),
            pltpu.VMEM((3 * half, 2 * rows), BF),
        ],
        compiler_params=pltpu.CompilerParams(vmem_limit_bytes=16 << 20),
        cost_estimate=pl.CostEstimate(
            flops=18 * channels * channels * rows,
            bytes_accessed=4 * rows * channels * 2 + 9 * channels * channels,
            transcendentals=0,
        ),
    )(act_a, act_b, dout_a, dout_b, turn)


def map_rows(images):
    h, w, n, c = images.shape
    return jnp.pad(images, ((0, 16 - h), (0, 16 - w), (0, 0), (0, 0))).reshape(256 * n, c)


def fetch_kernel(*refs):
    count = len(refs) // 2
    sems = refs[-1]
    copies = [
        pltpu.make_async_copy(refs[at], refs[count + at], sems.at[at]) for at in range(count)
    ]
    for copy in copies:
        copy.start()
    for copy in copies:
        copy.wait()


def fetch(values):
    anywhere = pl.BlockSpec(memory_space=pl.ANY)
    return pl.pallas_call(
        fetch_kernel,
        in_specs=[anywhere] * len(values),
        out_specs=[anywhere] * len(values),
        out_shape=[pltpu.VMEM(value.shape, value.dtype) for value in values],
        scratch_shapes=[pltpu.SemaphoreType.DMA((len(values),))],
        compiler_params=pltpu.CompilerParams(vmem_limit_bytes=56 << 20),
    )(*values)


def load_kernel(source, after, target, sems):
    del after
    rows = source.shape[0] // LOADS
    copies = [
        pltpu.make_async_copy(
            source.at[pl.ds(at * rows, rows)], target.at[pl.ds(at * rows, rows)], sems.at[at]
        )
        for at in range(LOADS)
    ]
    for copy in copies:
        copy.start()
    for copy in copies:
        copy.wait()


def load(value, after):
    return pl.pallas_call(
        load_kernel,
        in_specs=[pl.BlockSpec(memory_space=pl.ANY), pl.BlockSpec(memory_space=pltpu.VMEM)],
        out_specs=pl.BlockSpec(memory_space=pl.ANY),
        out_shape=pltpu.VMEM(value.shape, value.dtype),
        scratch_shapes=[pltpu.SemaphoreType.DMA((LOADS,))],
        compiler_params=pltpu.CompilerParams(vmem_limit_bytes=44 << 20),
        cost_estimate=pl.CostEstimate(flops=0, bytes_accessed=4 * value.size, transcendentals=0),
    )(value, after)


def stage(kernel, out_shape, operands, after=(), flops=0):
    near = pl.BlockSpec(memory_space=pltpu.VMEM)

    def body(*refs):
        kernel(refs[: len(operands)], refs[len(operands) + len(after) :])

    results = pl.pallas_call(
        body,
        in_specs=[near] * (len(operands) + len(after)),
        out_specs=[near] * len(out_shape),
        out_shape=out_shape,
        compiler_params=pltpu.CompilerParams(vmem_limit_bytes=8 << 20),
        cost_estimate=pl.CostEstimate(flops=flops, bytes_accessed=0, transcendentals=0),
    )(*operands, *after)
    return list(results)


def first_sum(ins, outs):
    kept, sent = outs[0], outs[1:]
    sub = sent[0].shape[0]
    for route in (0, 1):
        mine, came = ins[2 * route], ins[2 * route + 1]
        low, high = slice(0, sub), slice(sub, 2 * sub)
        kept[route * sub : (route + 1) * sub, :] = mine[low, :].astype(F32) + came[low, :].astype(
            F32
        )
        sent[route][...] = (mine[high, :].astype(F32) + came[high, :].astype(F32)).astype(BF)


def deal(value, outs, width, behind=None):
    me = lax.axis_index("grp")
    groups = len(outs)
    for step, out in enumerate(outs):
        at = pl.multiple_of(lax.rem(me + step, groups) * width, 128)
        out[:, 0:width] = value[:, pl.ds(at, width)].astype(out.dtype)
        if behind is not None:
            out[:, width:] = behind.astype(out.dtype)


def second_sum(ins, outs):
    *outs, total = outs
    sub = ins[1].shape[0]
    for at in (0, 1):
        kept, *others = ins[3 * at : 3 * at + 3]
        for route, came in enumerate(others):
            low = 2 * sub * at + route * sub
            total[low : low + sub, :] = kept[route * sub : (route + 1) * sub, :] + came[
                ...
            ].astype(F32)
    rows, width = outs[0].shape
    deal(total, outs, width - 128, total[:, len(outs) * (width - 128) :])


def gathered(ins):
    total = ins[0][...]
    for other in ins[1:]:
        total = total + other[...].astype(F32)
    return total


def prepare(ins, outs, images_all):
    sums = gathered(ins)
    rows = outs[0].shape[1]
    outs[0][...] = (sums[:, :rows] / images_all).astype(BF)
    outs[1][...] = sums[:, rows:]


def rotate(ins, outs, spans):
    columns, basis = ins
    me = lax.axis_index("grp")
    rows = basis.shape[0]
    groups = len(outs) // len(spans)
    for step in range(groups):
        at = pl.multiple_of(lax.rem(me + step, groups) * rows, 128)
        part = jnp.dot(columns[...], basis[:, pl.ds(at, rows)], preferred_element_type=F32)
        for c, (low, high) in enumerate(spans):
            out = outs[groups * c + step]
            out[...] = part[:, low:high].astype(BF).astype(out.dtype)


def rescale(ins, outs, positions, offset):
    *ins, moments, input_eigen = ins
    eigen_out = jnp.sum(moments[...], axis=1, keepdims=True) / positions
    chunk = outs[0].shape[1]
    scale = input_eigen[:, offset : offset + chunk] * eigen_out + damping
    outs[0][...] = (gathered(ins) / scale).astype(BF)


def turn_back(ins, outs):
    *near, weights = ins
    width = near[0].shape[0]
    total = None
    for at, block in enumerate(near):
        part = jnp.dot(
            weights[:, at * width : (at + 1) * width], block[...], preferred_element_type=F32
        )
        total = part if total is None else total + part
    outs[0][...] = total[:width]
    outs[1][...] = total[width:]


def merge(ins, outs):
    outs[0][...] = (ins[0][...] + ins[1][...]).astype(BF)


def restore(ins, outs, steps, offset, last):
    *blocks, basis = ins
    me = lax.axis_index("grp")
    rows = basis.shape[0]
    groups = basis.shape[1] // rows
    total = None
    if len(blocks) > len(steps):
        total = blocks.pop()[...]
    for step, block in zip(steps, blocks):
        chunk = block.shape[1]
        at = pl.multiple_of(lax.rem(me - step + groups, groups) * rows + offset, 128)
        part = lax.dot_general(
            block[...],
            basis[:, pl.ds(at, chunk)],
            (((1,), (1,)), ((), ())),
            preferred_element_type=F32,
        )
        total = part if total is None else total + part
    outs[0][...] = total.astype(outs[0].dtype)


def cube(activations, out_grads, input_basis, output_basis, input_eigen):
    channels = output_basis.shape[0]
    local_images, side = activations.shape[:2]
    images_all = local_images * lax.axis_size("dp") * lax.axis_size("grp")
    groups = lax.axis_size("grp")
    me = lax.axis_index("dp")
    width = channels // 8
    own_rows = input_eigen.shape[0]
    block = (me & 1) * 4 + (me >> 1)

    both = jnp.concatenate(
        [lax.dynamic_slice_in_dim(output_basis, r * width, width, 0) for r in (me, me ^ 1)], 0
    )
    weights = jnp.concatenate(
        [
            lax.dynamic_slice_in_dim(both, (block ^ flip) * width, width, 1)
            for flip in range(4)
        ],
        1,
    )

    act_own = activations.transpose(1, 2, 0, 3)
    dout_own = out_grads.transpose(1, 2, 0, 3)
    act_near, dout_near, basis_near = fetch([act_own, dout_own, output_basis])
    act_rows = [map_rows(act_near), map_rows(swap(act_own, 1))]
    dout_rows = [map_rows(dout_near), map_rows(swap(dout_own, 1))]
    parts = list(grad_parts(*act_rows, *dout_rows, basis_near))

    sub = width // 4
    wide = groups * own_rows + 128
    like = jax.ShapeDtypeStruct
    grp_types = [F32] + [BF] * (groups - 1)
    parts[1], weights = lax.optimization_barrier((parts[1], weights))
    came = [
        [parts[4 * c + 1], swap(parts[4 * c], 2), parts[4 * c + 3], swap(parts[4 * c + 2], 4)]
        for c in (0, 1)
    ]
    basis = load(input_basis, parts[0])
    sums = ()
    for c in (0, 1):
        shapes = [like((2 * sub, wide), F32)] + [like((sub, wide), BF)] * 2
        kept, s_a, s_b = sums = stage(first_sum, shapes, came[c], sums[1:2], WORK[0][c])
        came[c] = [kept, swap(s_a, 4), swap(s_b, 2)]
    shapes = [like((width, own_rows + 128), t) for t in grp_types] + [like((width, wide), F32)]
    own, *others = stage(second_sum, shapes, came[0] + came[1], (), WORK[1][0])[:groups]
    came = [own] + [shift(value, step + 1) for step, value in enumerate(others)]
    columns, moments = stage(
        functools.partial(prepare, images_all=images_all),
        [like((width, own_rows), BF), like((width, 128), F32)],
        came,
        (),
        WORK[1][1],
    )

    spans = ((0, own_rows // 128 // 2 * 128), (own_rows // 128 // 2 * 128, own_rows))
    eigen_row = input_eigen.reshape(1, own_rows)
    rotated = stage(
        functools.partial(rotate, spans=spans),
        [like((width, high - low), t) for low, high in spans for t in grp_types],
        [columns, basis],
        (),
        WORK[2][0],
    )
    came = []
    for c in (0, 1):
        own, *others = rotated[groups * c : groups * (c + 1)]
        came.append([own] + [shift(value, step + 1) for step, value in enumerate(others)])
    near, scaled = [], ()
    for (low, high), values in zip(spans, came):
        scaled = stage(
            functools.partial(rescale, positions=images_all * side * side, offset=low),
            [like((width, high - low), BF)],
            values + [moments, eigen_row],
            scaled,
            WORK[3][low > 0],
        )
        near.append(scaled + [swap(scaled[0], bit) for bit in (2, 4, 6)])
    held = []
    for (low, high), values in zip(spans, near):
        mine, sent = stage(
            turn_back,
            [like((width, high - low), F32)] * 2,
            values + [weights],
            (),
            WORK[4][low > 0],
        )
        (own,) = stage(merge, [like((width, high - low), BF)], [mine, swap(sent, 1)], (), WORK[5][low > 0])
        held.append([own] + [shift(own, step) for step in range(1, groups)])

    update = []
    calls = [(0, (0,)), (1, (0,)), (0, tuple(range(1, groups)))]
    calls += [(1, (step,)) for step in range(1, groups)]
    for at, (c, steps) in enumerate(calls):
        last = at == len(calls) - 1
        update = stage(
            functools.partial(restore, steps=steps, offset=spans[c][0], last=last),
            [like((width, own_rows), BF) if last else like((width, own_rows), F32)],
            [held[c][step] for step in steps] + update + [basis],
            (),
            len(steps) * WORK[6][c],
        )
    return update[0].T


def solution(mesh):
    in_specs = (
        P(("dp", "grp"), None, None, None),
        P(("dp", "grp"), None, None, None),
        P("grp", None),
        P(),
        P("grp"),
    )
    out_specs = P("grp", "dp")
    plan = cube if mesh.shape["dp"] == 8 else any_mesh
    return jax.shard_map(plan, mesh=mesh, in_specs=in_specs, out_specs=out_specs, check_vma=False)
```

```python
import functools

import jax
import jax.numpy as jnp
from jax import lax
from jax.experimental import pallas as pl
from jax.experimental.pallas import tpu as pltpu
from jax.sharding import PartitionSpec as P

damping = 1.0
BF = jnp.bfloat16
F32 = jnp.float32
WORK = [[0, 0], [400000000, 1000000000], [75000000, 75000000], [400000000, 0], [30000000, 150000000], [400000000, 1000000000], [400000000, 400000000], [0, 0], [300000000, 0]]
LOADS = 8


def unfold(images):
    side = images.shape[1]
    channels = images.shape[3]
    padded = jnp.pad(images, ((0, 0), (1, 1), (1, 1), (0, 0)))
    pieces = [
        padded[:, row : row + side, col : col + side, :] for row in range(3) for col in range(3)
    ]
    return jnp.concatenate(pieces, axis=-1).reshape(-1, 9 * channels)


def rounded(value):
    return lax.optimization_barrier(value.astype(jnp.bfloat16)).astype(jnp.float32)


def any_mesh(activations, out_grads, input_basis, output_basis, input_eigen):
    channels = output_basis.shape[0]
    side = activations.shape[1]
    local_images = activations.shape[0]
    replicas = lax.axis_size("dp")
    groups = lax.axis_size("grp")
    images_all = local_images * replicas * groups
    contract_rows = (((0,), (0,)), ((), ()))
    flat = out_grads.reshape(-1, channels)
    turned = jnp.dot(flat, output_basis, preferred_element_type=jnp.float32)
    turned_b = turned.astype(jnp.bfloat16)
    moment = rounded(jnp.sum(turned * turned, axis=0))
    patches = unfold(activations)
    term = lax.dot_general(patches, turned_b, contract_rows, preferred_element_type=jnp.float32)
    tiled = jnp.broadcast_to(moment[None, :], (groups, channels))
    group_sum, group_moment = (
        lax.psum_scatter(term.astype(jnp.bfloat16), "grp", scatter_dimension=0, tiled=True).astype(
            jnp.float32
        ),
        lax.psum_scatter(tiled.astype(jnp.bfloat16), "grp", scatter_dimension=0, tiled=True).astype(
            jnp.float32
        ),
    )
    grad_total, moment_rows = lax.psum((group_sum, group_moment), "dp")
    moment_total = moment_rows[0]
    grad_mean = (grad_total / images_all).astype(jnp.bfloat16)
    eigen_out = moment_total / (images_all * side * side)
    width = channels // replicas
    offset = lax.axis_index("dp") * width
    columns = lax.dynamic_slice_in_dim(grad_mean, offset, width, 1)
    rotated = lax.psum_scatter(
        lax.dot_general(
            input_basis, columns, contract_rows, preferred_element_type=jnp.float32
        ).astype(jnp.bfloat16),
        "grp",
        scatter_dimension=0,
        tiled=True,
    ).astype(jnp.float32)
    eigen_cols = lax.dynamic_slice_in_dim(eigen_out, offset, width, 0)
    scaled = (rotated / (input_eigen[:, None] * eigen_cols[None, :] + damping)).astype(jnp.bfloat16)
    back = jnp.dot(
        input_basis,
        lax.all_gather(scaled, "grp", axis=0, tiled=True),
        preferred_element_type=jnp.float32,
    )
    block = back.astype(jnp.bfloat16)
    out_rows = lax.dynamic_slice_in_dim(output_basis, offset, width, 0)
    final = lax.dot_general(
        lax.all_gather(block, "dp", axis=1, tiled=True),
        out_rows,
        (((1,), (1,)), ((), ())),
        preferred_element_type=jnp.float32,
    )
    return final.astype(jnp.bfloat16)


def swap(value, bit):
    return lax.ppermute(value, "dp", [(i, i ^ bit) for i in range(lax.axis_size("dp"))])


def shift(value, step):
    n = lax.axis_size("grp")
    return lax.ppermute(value, "grp", [(i, (i + step) % n) for i in range(n)])


ROUTES = (((1, 3), (0, 2)), ((2, 3), (0, 1)))
ORDER = tuple(
    (2 * chunk + route, flip)
    for chunk in (0, 1)
    for route in (0, 1)
    for flips in ROUTES[route]
    for flip in flips
)


def grad_kernel(act_a, act_b, dout_a, dout_b, turn, *refs):
    pieces, (acts, flipped, turned, lhs) = refs[:8], refs[8:]
    rows, channels = act_a.shape
    edge = rows // 16
    images = edge // 16
    half = channels // 2
    sub = half // len(ORDER)
    me = lax.axis_index("dp")
    quarter = me >> 1
    flipped[...] = turn[:, pl.ds(pl.multiple_of((me & 1) * half, half), half)].T
    for at, (part, flip) in enumerate(ORDER):
        start = pl.multiple_of((quarter ^ flip) * 4 * sub + part * sub, sub)
        turned[at * sub : (at + 1) * sub, :] = flipped[pl.ds(start, sub), :]
    acts[0:edge, :] = jnp.zeros((edge, channels), BF)
    acts[edge + 2 * rows :, :] = jnp.zeros((edge, channels), BF)
    acts[edge : edge + rows, :] = act_a[...]
    acts[edge + rows : edge + 2 * rows, :] = act_b[...]
    squares = jnp.zeros((half, 128), F32)
    for at, ref in enumerate((dout_a, dout_b)):
        part = lax.dot_general(
            turned[...], ref[...], (((1,), (1,)), ((), ())), preferred_element_type=F32
        )
        for lane in range(0, rows, 128):
            squares = squares + part[:, lane : lane + 128] * part[:, lane : lane + 128]
        for tap, by in enumerate((rows - images, 0, images)):
            moved = pltpu.roll(part, by, 1) if by else part
            lhs[tap * half : (tap + 1) * half, at * rows : (at + 1) * rows] = moved.astype(BF)
    for at, ref in enumerate(pieces):
        ref[:, 9 * channels :] = squares[at * 2 * sub : (at + 1) * 2 * sub, :].astype(BF)
    for step in range(3):
        window = acts[edge * step : edge * step + 2 * rows, :]
        out = jnp.dot(lhs[...], window, preferred_element_type=F32)
        for tap in range(3):
            column = (3 * step + tap) * channels
            for at, ref in enumerate(pieces):
                start = tap * half + at * 2 * sub
                ref[:, column : column + channels] = out[start : start + 2 * sub, :].astype(BF)


def grad_parts(act_a, act_b, dout_a, dout_b, turn):
    rows, channels = act_a.shape
    half = channels // 2
    near = pl.BlockSpec(memory_space=pltpu.VMEM)
    return pl.pallas_call(
        grad_kernel,
        in_specs=[near] * 5,
        out_specs=[near] * 8,
        out_shape=[jax.ShapeDtypeStruct((half // 8, 9 * channels + 128), BF)] * 8,
        scratch_shapes=[
            pltpu.VMEM((2 * rows + rows // 8, channels), BF),
            pltpu.VMEM((half, channels), BF),
            pltpu.VMEM((half, channels), BF),
            pltpu.VMEM((3 * half, 2 * rows), BF),
        ],
        compiler_params=pltpu.CompilerParams(vmem_limit_bytes=16 << 20),
        cost_estimate=pl.CostEstimate(
            flops=18 * channels * channels * rows,
            bytes_accessed=4 * rows * channels * 2 + 9 * channels * channels,
            transcendentals=0,
        ),
    )(act_a, act_b, dout_a, dout_b, turn)


def map_rows(images):
    h, w, n, c = images.shape
    return jnp.pad(images, ((0, 16 - h), (0, 16 - w), (0, 0), (0, 0))).reshape(256 * n, c)


def fetch_kernel(*refs):
    count = len(refs) // 2
    sems = refs[-1]
    copies = [
        pltpu.make_async_copy(refs[at], refs[count + at], sems.at[at]) for at in range(count)
    ]
    for copy in copies:
        copy.start()
    for copy in copies:
        copy.wait()


def fetch(values):
    anywhere = pl.BlockSpec(memory_space=pl.ANY)
    return pl.pallas_call(
        fetch_kernel,
        in_specs=[anywhere] * len(values),
        out_specs=[anywhere] * len(values),
        out_shape=[pltpu.VMEM(value.shape, value.dtype) for value in values],
        scratch_shapes=[pltpu.SemaphoreType.DMA((len(values),))],
        compiler_params=pltpu.CompilerParams(vmem_limit_bytes=56 << 20),
    )(*values)


def load_kernel(source, after, target, sems):
    del after
    rows = source.shape[0] // LOADS
    copies = [
        pltpu.make_async_copy(
            source.at[pl.ds(at * rows, rows)], target.at[pl.ds(at * rows, rows)], sems.at[at]
        )
        for at in range(LOADS)
    ]
    for copy in copies:
        copy.start()
    for copy in copies:
        copy.wait()


def load(value, after):
    return pl.pallas_call(
        load_kernel,
        in_specs=[pl.BlockSpec(memory_space=pl.ANY), pl.BlockSpec(memory_space=pltpu.VMEM)],
        out_specs=pl.BlockSpec(memory_space=pl.ANY),
        out_shape=pltpu.VMEM(value.shape, value.dtype),
        scratch_shapes=[pltpu.SemaphoreType.DMA((LOADS,))],
        compiler_params=pltpu.CompilerParams(vmem_limit_bytes=44 << 20),
        cost_estimate=pl.CostEstimate(flops=0, bytes_accessed=4 * value.size, transcendentals=0),
    )(value, after)


def stage(kernel, out_shape, operands, after=(), flops=0):
    near = pl.BlockSpec(memory_space=pltpu.VMEM)

    def body(*refs):
        kernel(refs[: len(operands)], refs[len(operands) + len(after) :])

    results = pl.pallas_call(
        body,
        in_specs=[near] * (len(operands) + len(after)),
        out_specs=[near] * len(out_shape),
        out_shape=out_shape,
        compiler_params=pltpu.CompilerParams(vmem_limit_bytes=8 << 20),
        cost_estimate=pl.CostEstimate(flops=flops, bytes_accessed=0, transcendentals=0),
    )(*operands, *after)
    return list(results)


def first_sum(ins, outs):
    kept, sent = outs[0], outs[1:]
    sub = sent[0].shape[0]
    for route in (0, 1):
        mine, came = ins[2 * route], ins[2 * route + 1]
        low, high = slice(0, sub), slice(sub, 2 * sub)
        kept[route * sub : (route + 1) * sub, :] = mine[low, :].astype(F32) + came[low, :].astype(
            F32
        )
        sent[route][...] = (mine[high, :].astype(F32) + came[high, :].astype(F32)).astype(BF)


def second_sum(ins, outs):
    *outs, total = outs
    kept, came_a, came_b = ins
    sub = came_a.shape[0]
    for route, came in enumerate((came_a, came_b)):
        rows = slice(route * sub, (route + 1) * sub)
        total[rows, :] = kept[rows, :] + came[...].astype(F32)
    width = outs[0].shape[1] - 128
    me = lax.axis_index("grp")
    groups = len(outs)
    rest = total[:, groups * width :]
    for step, out in enumerate(outs):
        at = pl.multiple_of(lax.rem(me + step, groups) * width, 128)
        out[:, 0:width] = total[:, pl.ds(at, width)].astype(out.dtype)
        out[:, width:] = rest.astype(out.dtype)


def gathered(ins):
    total = ins[0][...]
    for other in ins[1:]:
        total = total + other[...].astype(F32)
    return total


def prepare(ins, outs, images_all, groups):
    columns, moments = outs
    low, rows = columns.shape
    sums = gathered(ins[len(ins) - groups :])
    low -= sums.shape[0]
    for ref, earlier in zip(outs, ins[: len(ins) - groups]):
        ref[:low, :] = earlier[...]
    columns[low:, :] = (sums[:, :rows] / images_all).astype(BF)
    moments[low:, :] = sums[:, rows:]


def rotate(ins, outs, spans):
    columns, basis = ins
    me = lax.axis_index("grp")
    rows = basis.shape[0]
    groups = len(outs) // len(spans)
    for step in range(groups):
        at = pl.multiple_of(lax.rem(me + step, groups) * rows, 128)
        part = jnp.dot(columns[...], basis[:, pl.ds(at, rows)], preferred_element_type=F32)
        for c, (low, high) in enumerate(spans):
            out = outs[groups * c + step]
            out[...] = part[:, low:high].astype(BF).astype(out.dtype)


def rescale(ins, outs, positions, offset):
    *ins, moments, input_eigen = ins
    eigen_out = jnp.sum(moments[...], axis=1, keepdims=True) / positions
    chunk = outs[0].shape[1]
    scale = input_eigen[:, offset : offset + chunk] * eigen_out + damping
    outs[0][...] = (gathered(ins) / scale).astype(BF)


def turn_back(ins, outs):
    *near, weights = ins
    width = near[0].shape[0]
    total = None
    for at, block in enumerate(near):
        part = jnp.dot(
            weights[:, at * width : (at + 1) * width], block[...], preferred_element_type=F32
        )
        total = part if total is None else total + part
    outs[0][...] = total[:width]
    outs[1][...] = total[width:]


def merge(ins, outs):
    outs[0][...] = (ins[0][...] + ins[1][...]).astype(BF)


def restore(ins, outs, steps, offset, last):
    *blocks, basis = ins
    me = lax.axis_index("grp")
    rows = basis.shape[0]
    groups = basis.shape[1] // rows
    total = None
    if len(blocks) > len(steps):
        total = blocks.pop()[...]
    for step, block in zip(steps, blocks):
        chunk = block.shape[1]
        at = pl.multiple_of(lax.rem(me - step + groups, groups) * rows + offset, 128)
        part = lax.dot_general(
            block[...],
            basis[:, pl.ds(at, chunk)],
            (((1,), (1,)), ((), ())),
            preferred_element_type=F32,
        )
        total = part if total is None else total + part
    outs[0][...] = total.astype(outs[0].dtype)


def cube(activations, out_grads, input_basis, output_basis, input_eigen):
    channels = output_basis.shape[0]
    local_images, side = activations.shape[:2]
    images_all = local_images * lax.axis_size("dp") * lax.axis_size("grp")
    groups = lax.axis_size("grp")
    me = lax.axis_index("dp")
    width = channels // 8
    own_rows = input_eigen.shape[0]
    block = (me & 1) * 4 + (me >> 1)

    both = jnp.concatenate(
        [lax.dynamic_slice_in_dim(output_basis, r * width, width, 0) for r in (me, me ^ 1)], 0
    )
    weights = jnp.concatenate(
        [
            lax.dynamic_slice_in_dim(both, (block ^ flip) * width, width, 1)
            for flip in range(4)
        ],
        1,
    )

    act_own = activations.transpose(1, 2, 0, 3)
    dout_own = out_grads.transpose(1, 2, 0, 3)
    act_near, dout_near, basis_near = fetch([act_own, dout_own, output_basis])
    act_rows = [map_rows(act_near), map_rows(swap(act_own, 1))]
    dout_rows = [map_rows(dout_near), map_rows(swap(dout_own, 1))]
    parts = list(grad_parts(*act_rows, *dout_rows, basis_near))

    sub = width // 4
    wide = groups * own_rows + 128
    like = jax.ShapeDtypeStruct
    grp_types = [F32] + [BF] * (groups - 1)
    parts[1], weights = lax.optimization_barrier((parts[1], weights))
    came = [
        [parts[4 * c + 1], swap(parts[4 * c], 2), parts[4 * c + 3], swap(parts[4 * c + 2], 4)]
        for c in (0, 1)
    ]
    basis = load(input_basis, parts[0])
    sums = ()
    for c in (0, 1):
        shapes = [like((2 * sub, wide), F32)] + [like((sub, wide), BF)] * 2
        kept, s_a, s_b = sums = stage(first_sum, shapes, came[c], sums[1:2], WORK[0][c])
        came[c] = [kept, swap(s_a, 4), swap(s_b, 2)]
    held = []
    for c in (0, 1):
        shapes = [like((2 * sub, own_rows + 128), t) for t in grp_types] + [like((2 * sub, wide), F32)]
        own, *others = stage(second_sum, shapes, came[c], (), WORK[7][c])[:groups]
        came[c] = [own] + [shift(value, step + 1) for step, value in enumerate(others)]
    for c in (0, 1):
        rows = 2 * sub * (c + 1)
        held = stage(
            functools.partial(prepare, images_all=images_all, groups=groups),
            [like((rows, own_rows), BF), like((rows, 128), F32)],
            held + came[c],
            (),
            WORK[8][c],
        )
    columns, moments = held

    spans = ((0, own_rows // 128 // 2 * 128), (own_rows // 128 // 2 * 128, own_rows))
    eigen_row = input_eigen.reshape(1, own_rows)
    rotated = stage(
        functools.partial(rotate, spans=spans),
        [like((width, high - low), t) for low, high in spans for t in grp_types],
        [columns, basis],
        (),
        WORK[2][0],
    )
    came = []
    for c in (0, 1):
        own, *others = rotated[groups * c : groups * (c + 1)]
        came.append([own] + [shift(value, step + 1) for step, value in enumerate(others)])
    near, scaled = [], ()
    for (low, high), values in zip(spans, came):
        scaled = stage(
            functools.partial(rescale, positions=images_all * side * side, offset=low),
            [like((width, high - low), BF)],
            values + [moments, eigen_row],
            scaled,
            WORK[3][low > 0],
        )
        near.append(scaled + [swap(scaled[0], bit) for bit in (2, 4, 6)])
    held = []
    for (low, high), values in zip(spans, near):
        mine, sent = stage(
            turn_back,
            [like((width, high - low), F32)] * 2,
            values + [weights],
            (),
            WORK[4][low > 0],
        )
        (own,) = stage(merge, [like((width, high - low), BF)], [mine, swap(sent, 1)], (), WORK[5][low > 0])
        held.append([own] + [shift(own, step) for step in range(1, groups)])

    update = []
    calls = [(0, (0,)), (1, (0,)), (0, tuple(range(1, groups)))]
    calls += [(1, (step,)) for step in range(1, groups)]
    for at, (c, steps) in enumerate(calls):
        last = at == len(calls) - 1
        update = stage(
            functools.partial(restore, steps=steps, offset=spans[c][0], last=last),
            [like((width, own_rows), BF) if last else like((width, own_rows), F32)],
            [held[c][step] for step in steps] + update + [basis],
            (),
            len(steps) * WORK[6][c],
        )
    return update[0].T


def solution(mesh):
    in_specs = (
        P(("dp", "grp"), None, None, None),
        P(("dp", "grp"), None, None, None),
        P("grp", None),
        P(),
        P("grp"),
    )
    out_specs = P("grp", "dp")
    plan = cube if mesh.shape["dp"] == 8 else any_mesh
    return jax.shard_map(plan, mesh=mesh, in_specs=in_specs, out_specs=out_specs, check_vma=False)
```

```python
import functools

import jax
import jax.numpy as jnp
from jax import lax
from jax.experimental import pallas as pl
from jax.experimental.pallas import tpu as pltpu
from jax.sharding import PartitionSpec as P

damping = 1.0
BF = jnp.bfloat16
F32 = jnp.float32
WORK = [[0, 0], [400000000, 1000000000], [75000000, 75000000], [400000000, 0], [30000000, 150000000], [0, 0], [1000000000, 100000000], [0, 0], [300000000, 0]]
LOADS = 8


def unfold(images):
    side = images.shape[1]
    channels = images.shape[3]
    padded = jnp.pad(images, ((0, 0), (1, 1), (1, 1), (0, 0)))
    pieces = [
        padded[:, row : row + side, col : col + side, :] for row in range(3) for col in range(3)
    ]
    return jnp.concatenate(pieces, axis=-1).reshape(-1, 9 * channels)


def rounded(value):
    return lax.optimization_barrier(value.astype(jnp.bfloat16)).astype(jnp.float32)


def any_mesh(activations, out_grads, input_basis, output_basis, input_eigen):
    channels = output_basis.shape[0]
    side = activations.shape[1]
    local_images = activations.shape[0]
    replicas = lax.axis_size("dp")
    groups = lax.axis_size("grp")
    images_all = local_images * replicas * groups
    contract_rows = (((0,), (0,)), ((), ()))
    flat = out_grads.reshape(-1, channels)
    turned = jnp.dot(flat, output_basis, preferred_element_type=jnp.float32)
    turned_b = turned.astype(jnp.bfloat16)
    moment = rounded(jnp.sum(turned * turned, axis=0))
    patches = unfold(activations)
    term = lax.dot_general(patches, turned_b, contract_rows, preferred_element_type=jnp.float32)
    tiled = jnp.broadcast_to(moment[None, :], (groups, channels))
    group_sum, group_moment = (
        lax.psum_scatter(term.astype(jnp.bfloat16), "grp", scatter_dimension=0, tiled=True).astype(
            jnp.float32
        ),
        lax.psum_scatter(tiled.astype(jnp.bfloat16), "grp", scatter_dimension=0, tiled=True).astype(
            jnp.float32
        ),
    )
    grad_total, moment_rows = lax.psum((group_sum, group_moment), "dp")
    moment_total = moment_rows[0]
    grad_mean = (grad_total / images_all).astype(jnp.bfloat16)
    eigen_out = moment_total / (images_all * side * side)
    width = channels // replicas
    offset = lax.axis_index("dp") * width
    columns = lax.dynamic_slice_in_dim(grad_mean, offset, width, 1)
    rotated = lax.psum_scatter(
        lax.dot_general(
            input_basis, columns, contract_rows, preferred_element_type=jnp.float32
        ).astype(jnp.bfloat16),
        "grp",
        scatter_dimension=0,
        tiled=True,
    ).astype(jnp.float32)
    eigen_cols = lax.dynamic_slice_in_dim(eigen_out, offset, width, 0)
    scaled = (rotated / (input_eigen[:, None] * eigen_cols[None, :] + damping)).astype(jnp.bfloat16)
    back = jnp.dot(
        input_basis,
        lax.all_gather(scaled, "grp", axis=0, tiled=True),
        preferred_element_type=jnp.float32,
    )
    block = back.astype(jnp.bfloat16)
    out_rows = lax.dynamic_slice_in_dim(output_basis, offset, width, 0)
    final = lax.dot_general(
        lax.all_gather(block, "dp", axis=1, tiled=True),
        out_rows,
        (((1,), (1,)), ((), ())),
        preferred_element_type=jnp.float32,
    )
    return final.astype(jnp.bfloat16)


def swap(value, bit):
    return lax.ppermute(value, "dp", [(i, i ^ bit) for i in range(lax.axis_size("dp"))])


def shift(value, step):
    n = lax.axis_size("grp")
    return lax.ppermute(value, "grp", [(i, (i + step) % n) for i in range(n)])


ROUTES = (((1, 3), (0, 2)), ((2, 3), (0, 1)))
ORDER = tuple(
    (2 * chunk + route, flip)
    for chunk in (0, 1)
    for route in (0, 1)
    for flips in ROUTES[route]
    for flip in flips
)


def grad_kernel(act_a, act_b, dout_a, dout_b, turn, *refs):
    pieces, (acts, flipped, turned, lhs) = refs[:8], refs[8:]
    rows, channels = act_a.shape
    edge = rows // 16
    images = edge // 16
    half = channels // 2
    sub = half // len(ORDER)
    me = lax.axis_index("dp")
    quarter = me >> 1
    flipped[...] = turn[:, pl.ds(pl.multiple_of((me & 1) * half, half), half)].T
    for at, (part, flip) in enumerate(ORDER):
        start = pl.multiple_of((quarter ^ flip) * 4 * sub + part * sub, sub)
        turned[at * sub : (at + 1) * sub, :] = flipped[pl.ds(start, sub), :]
    acts[0:edge, :] = jnp.zeros((edge, channels), BF)
    acts[edge + 2 * rows :, :] = jnp.zeros((edge, channels), BF)
    acts[edge : edge + rows, :] = act_a[...]
    acts[edge + rows : edge + 2 * rows, :] = act_b[...]
    squares = jnp.zeros((half, 128), F32)
    for at, ref in enumerate((dout_a, dout_b)):
        part = lax.dot_general(
            turned[...], ref[...], (((1,), (1,)), ((), ())), preferred_element_type=F32
        )
        for lane in range(0, rows, 128):
            squares = squares + part[:, lane : lane + 128] * part[:, lane : lane + 128]
        for tap, by in enumerate((rows - images, 0, images)):
            moved = pltpu.roll(part, by, 1) if by else part
            lhs[tap * half : (tap + 1) * half, at * rows : (at + 1) * rows] = moved.astype(BF)
    for at, ref in enumerate(pieces):
        ref[:, 9 * channels :] = squares[at * 2 * sub : (at + 1) * 2 * sub, :].astype(BF)
    for step in range(3):
        window = acts[edge * step : edge * step + 2 * rows, :]
        out = jnp.dot(lhs[...], window, preferred_element_type=F32)
        for tap in range(3):
            column = (3 * step + tap) * channels
            for at, ref in enumerate(pieces):
                start = tap * half + at * 2 * sub
                ref[:, column : column + channels] = out[start : start + 2 * sub, :].astype(BF)


def grad_parts(act_a, act_b, dout_a, dout_b, turn):
    rows, channels = act_a.shape
    half = channels // 2
    near = pl.BlockSpec(memory_space=pltpu.VMEM)
    return pl.pallas_call(
        grad_kernel,
        in_specs=[near] * 5,
        out_specs=[near] * 8,
        out_shape=[jax.ShapeDtypeStruct((half // 8, 9 * channels + 128), BF)] * 8,
        scratch_shapes=[
            pltpu.VMEM((2 * rows + rows // 8, channels), BF),
            pltpu.VMEM((half, channels), BF),
            pltpu.VMEM((half, channels), BF),
            pltpu.VMEM((3 * half, 2 * rows), BF),
        ],
        compiler_params=pltpu.CompilerParams(vmem_limit_bytes=16 << 20),
        cost_estimate=pl.CostEstimate(
            flops=18 * channels * channels * rows,
            bytes_accessed=4 * rows * channels * 2 + 9 * channels * channels,
            transcendentals=0,
        ),
    )(act_a, act_b, dout_a, dout_b, turn)


def map_rows(images):
    h, w, n, c = images.shape
    rows = images.reshape(h, w * n, c)
    return jnp.pad(rows, ((0, 16 - h), (0, (16 - w) * n), (0, 0))).reshape(256 * n, c)


def fetch_kernel(*refs):
    count = len(refs) // 2
    sems = refs[-1]
    copies = [
        pltpu.make_async_copy(refs[at], refs[count + at], sems.at[at]) for at in range(count)
    ]
    for copy in copies:
        copy.start()
    for copy in copies:
        copy.wait()


def fetch(values):
    anywhere = pl.BlockSpec(memory_space=pl.ANY)
    return pl.pallas_call(
        fetch_kernel,
        in_specs=[anywhere] * len(values),
        out_specs=[anywhere] * len(values),
        out_shape=[pltpu.VMEM(value.shape, value.dtype) for value in values],
        scratch_shapes=[pltpu.SemaphoreType.DMA((len(values),))],
        compiler_params=pltpu.CompilerParams(vmem_limit_bytes=56 << 20),
    )(*values)


def load_kernel(source, after, target, sems):
    del after
    rows = source.shape[0] // LOADS
    copies = [
        pltpu.make_async_copy(
            source.at[pl.ds(at * rows, rows)], target.at[pl.ds(at * rows, rows)], sems.at[at]
        )
        for at in range(LOADS)
    ]
    for copy in copies:
        copy.start()
    for copy in copies:
        copy.wait()


def load(value, after):
    return pl.pallas_call(
        load_kernel,
        in_specs=[pl.BlockSpec(memory_space=pl.ANY), pl.BlockSpec(memory_space=pltpu.VMEM)],
        out_specs=pl.BlockSpec(memory_space=pl.ANY),
        out_shape=pltpu.VMEM(value.shape, value.dtype),
        scratch_shapes=[pltpu.SemaphoreType.DMA((LOADS,))],
        compiler_params=pltpu.CompilerParams(vmem_limit_bytes=44 << 20),
        cost_estimate=pl.CostEstimate(flops=0, bytes_accessed=4 * value.size, transcendentals=0),
    )(value, after)


def stage(kernel, out_shape, operands, after=(), flops=0):
    near = pl.BlockSpec(memory_space=pltpu.VMEM)

    def body(*refs):
        kernel(refs[: len(operands)], refs[len(operands) + len(after) :])

    results = pl.pallas_call(
        body,
        in_specs=[near] * (len(operands) + len(after)),
        out_specs=[near] * len(out_shape),
        out_shape=out_shape,
        compiler_params=pltpu.CompilerParams(vmem_limit_bytes=8 << 20),
        cost_estimate=pl.CostEstimate(flops=flops, bytes_accessed=0, transcendentals=0),
    )(*operands, *after)
    return list(results)


def first_sum(ins, outs):
    kept, sent = outs[0], outs[1:]
    sub = sent[0].shape[0]
    for route in (0, 1):
        mine, came = ins[2 * route], ins[2 * route + 1]
        low, high = slice(0, sub), slice(sub, 2 * sub)
        kept[route * sub : (route + 1) * sub, :] = mine[low, :].astype(F32) + came[low, :].astype(
            F32
        )
        sent[route][...] = (mine[high, :].astype(F32) + came[high, :].astype(F32)).astype(BF)


def second_sum(ins, outs):
    *outs, total = outs
    kept, came_a, came_b = ins
    sub = came_a.shape[0]
    for route, came in enumerate((came_a, came_b)):
        rows = slice(route * sub, (route + 1) * sub)
        total[rows, :] = kept[rows, :] + came[...].astype(F32)
    width = outs[0].shape[1] - 128
    me = lax.axis_index("grp")
    groups = len(outs)
    rest = total[:, groups * width :]
    for step, out in enumerate(outs):
        at = pl.multiple_of(lax.rem(me + step, groups) * width, 128)
        out[:, 0:width] = total[:, pl.ds(at, width)].astype(out.dtype)
        out[:, width:] = rest.astype(out.dtype)


def gathered(ins):
    total = ins[0][...]
    for other in ins[1:]:
        total = total + other[...].astype(F32)
    return total


def prepare(ins, outs, images_all, groups):
    columns, moments = outs
    low, rows = columns.shape
    sums = gathered(ins[len(ins) - groups :])
    low -= sums.shape[0]
    for ref, earlier in zip(outs, ins[: len(ins) - groups]):
        ref[:low, :] = earlier[...]
    columns[low:, :] = (sums[:, :rows] / images_all).astype(BF)
    moments[low:, :] = sums[:, rows:]


def rotate(ins, outs, spans):
    columns, basis = ins
    me = lax.axis_index("grp")
    rows = basis.shape[0]
    groups = len(outs) // len(spans)
    for step in range(groups):
        at = pl.multiple_of(lax.rem(me + step, groups) * rows, 128)
        part = jnp.dot(columns[...], basis[:, pl.ds(at, rows)], preferred_element_type=F32)
        for c, (low, high) in enumerate(spans):
            out = outs[groups * c + step]
            out[...] = part[:, low:high].astype(BF).astype(out.dtype)


def rescale(ins, outs, positions, offset):
    *ins, moments, input_eigen = ins
    eigen_out = jnp.sum(moments[...], axis=1, keepdims=True) / positions
    chunk = outs[0].shape[1]
    scale = input_eigen[:, offset : offset + chunk] * eigen_out + damping
    outs[0][...] = (gathered(ins) / scale).astype(BF)


def turn_back(ins, outs):
    *near, weights = ins
    width = near[0].shape[0]
    total = None
    for at, block in enumerate(near):
        part = jnp.dot(
            weights[:, at * width : (at + 1) * width], block[...], preferred_element_type=F32
        )
        total = part if total is None else total + part
    outs[0][...] = total[:width]
    outs[1][...] = total[width:]


def merge(ins, outs):
    outs[0][...] = (ins[0][...] + ins[1][...]).astype(BF)


def restore(ins, outs, steps, offset, last):
    *blocks, basis = ins
    me = lax.axis_index("grp")
    rows = basis.shape[0]
    groups = basis.shape[1] // rows
    total = None
    if len(blocks) > len(steps):
        total = blocks.pop()[...]
    for step, block in zip(steps, blocks):
        chunk = block.shape[1]
        at = pl.multiple_of(lax.rem(me - step + groups, groups) * rows + offset, 128)
        part = lax.dot_general(
            block[...],
            basis[:, pl.ds(at, chunk)],
            (((1,), (1,)), ((), ())),
            preferred_element_type=F32,
        )
        total = part if total is None else total + part
    outs[0][...] = total.astype(outs[0].dtype)


def cube(activations, out_grads, input_basis, output_basis, input_eigen):
    channels = output_basis.shape[0]
    local_images, side = activations.shape[:2]
    images_all = local_images * lax.axis_size("dp") * lax.axis_size("grp")
    groups = lax.axis_size("grp")
    me = lax.axis_index("dp")
    width = channels // 8
    own_rows = input_eigen.shape[0]
    block = (me & 1) * 4 + (me >> 1)

    both = jnp.concatenate(
        [lax.dynamic_slice_in_dim(output_basis, r * width, width, 0) for r in (me, me ^ 1)], 0
    )
    weights = jnp.concatenate(
        [
            lax.dynamic_slice_in_dim(both, (block ^ flip) * width, width, 1)
            for flip in range(4)
        ],
        1,
    )

    act_own = activations.transpose(1, 2, 0, 3)
    dout_own = out_grads.transpose(1, 2, 0, 3)
    act_near, dout_near, basis_near = fetch([act_own, dout_own, output_basis])
    act_rows = [map_rows(act_near), map_rows(swap(act_own, 1))]
    dout_rows = [map_rows(dout_near), map_rows(swap(dout_own, 1))]
    parts = list(grad_parts(*act_rows, *dout_rows, basis_near))

    sub = width // 4
    wide = groups * own_rows + 128
    like = jax.ShapeDtypeStruct
    grp_types = [F32] + [BF] * (groups - 1)
    parts[1], weights = lax.optimization_barrier((parts[1], weights))
    came = [
        [parts[4 * c + 1], swap(parts[4 * c], 2), parts[4 * c + 3], swap(parts[4 * c + 2], 4)]
        for c in (0, 1)
    ]
    basis = load(input_basis, parts[0])
    sums = ()
    for c in (0, 1):
        shapes = [like((2 * sub, wide), F32)] + [like((sub, wide), BF)] * 2
        kept, s_a, s_b = sums = stage(first_sum, shapes, came[c], sums[1:2], WORK[0][c])
        came[c] = [kept, swap(s_a, 4), swap(s_b, 2)]
    held = []
    for c in (0, 1):
        shapes = [like((2 * sub, own_rows + 128), t) for t in grp_types] + [like((2 * sub, wide), F32)]
        own, *others = stage(second_sum, shapes, came[c], (), WORK[7][c])[:groups]
        came[c] = [own] + [shift(value, step + 1) for step, value in enumerate(others)]
    for c in (0, 1):
        rows = 2 * sub * (c + 1)
        held = stage(
            functools.partial(prepare, images_all=images_all, groups=groups),
            [like((rows, own_rows), BF), like((rows, 128), F32)],
            held + came[c],
            (),
            WORK[8][c],
        )
    columns, moments = held

    spans = ((0, own_rows // 128 // 2 * 128), (own_rows // 128 // 2 * 128, own_rows))
    eigen_row = input_eigen.reshape(1, own_rows)
    rotated = stage(
        functools.partial(rotate, spans=spans),
        [like((width, high - low), t) for low, high in spans for t in grp_types],
        [columns, basis],
        (),
        WORK[2][0],
    )
    came = []
    for c in (0, 1):
        own, *others = rotated[groups * c : groups * (c + 1)]
        came.append([own] + [shift(value, step + 1) for step, value in enumerate(others)])
    near, scaled = [], ()
    for (low, high), values in zip(spans, came):
        scaled = stage(
            functools.partial(rescale, positions=images_all * side * side, offset=low),
            [like((width, high - low), BF)],
            values + [moments, eigen_row],
            scaled,
            WORK[3][low > 0],
        )
        near.append(scaled + [swap(scaled[0], bit) for bit in (2, 4, 6)])
    held = []
    for (low, high), values in zip(spans, near):
        mine, sent = stage(
            turn_back,
            [like((width, high - low), F32)] * 2,
            values + [weights],
            (),
            WORK[4][low > 0],
        )
        (own,) = stage(merge, [like((width, high - low), BF)], [mine, swap(sent, 1)], (), WORK[5][low > 0])
        held.append([own] + [shift(own, step) for step in range(1, groups)])

    update = []
    calls = [(0, (0,)), (1, (0,)), (0, tuple(range(1, groups)))]
    calls += [(1, (step,)) for step in range(1, groups)]
    for at, (c, steps) in enumerate(calls):
        last = at == len(calls) - 1
        update = stage(
            functools.partial(restore, steps=steps, offset=spans[c][0], last=last),
            [like((width, own_rows), BF) if last else like((width, own_rows), F32)],
            [held[c][step] for step in steps] + update + [basis],
            (),
            len(steps) * WORK[6][c],
        )
    return update[0].T


def solution(mesh):
    in_specs = (
        P(("dp", "grp"), None, None, None),
        P(("dp", "grp"), None, None, None),
        P("grp", None),
        P(),
        P("grp"),
    )
    out_specs = P("grp", "dp")
    plan = cube if mesh.shape["dp"] == 8 else any_mesh
    return jax.shard_map(plan, mesh=mesh, in_specs=in_specs, out_specs=out_specs, check_vma=False)
```

```python
import functools

import jax
import jax.numpy as jnp
from jax import lax
from jax.experimental import pallas as pl
from jax.experimental.pallas import tpu as pltpu
from jax.sharding import PartitionSpec as P

damping = 1.0
BF = jnp.bfloat16
F32 = jnp.float32
WORK = [[0, 0], [400000000, 1000000000], [75000000, 75000000], [400000000, 0], [30000000, 150000000], [0, 0], [1000000000, 100000000], [0, 0], [300000000, 0]]
LOADS = 8


def unfold(images):
    side = images.shape[1]
    channels = images.shape[3]
    padded = jnp.pad(images, ((0, 0), (1, 1), (1, 1), (0, 0)))
    pieces = [
        padded[:, row : row + side, col : col + side, :] for row in range(3) for col in range(3)
    ]
    return jnp.concatenate(pieces, axis=-1).reshape(-1, 9 * channels)


def rounded(value):
    return lax.optimization_barrier(value.astype(jnp.bfloat16)).astype(jnp.float32)


def any_mesh(activations, out_grads, input_basis, output_basis, input_eigen):
    channels = output_basis.shape[0]
    side = activations.shape[1]
    local_images = activations.shape[0]
    replicas = lax.axis_size("dp")
    groups = lax.axis_size("grp")
    images_all = local_images * replicas * groups
    contract_rows = (((0,), (0,)), ((), ()))
    flat = out_grads.reshape(-1, channels)
    turned = jnp.dot(flat, output_basis, preferred_element_type=jnp.float32)
    turned_b = turned.astype(jnp.bfloat16)
    moment = rounded(jnp.sum(turned * turned, axis=0))
    patches = unfold(activations)
    term = lax.dot_general(patches, turned_b, contract_rows, preferred_element_type=jnp.float32)
    tiled = jnp.broadcast_to(moment[None, :], (groups, channels))
    group_sum, group_moment = (
        lax.psum_scatter(term.astype(jnp.bfloat16), "grp", scatter_dimension=0, tiled=True).astype(
            jnp.float32
        ),
        lax.psum_scatter(tiled.astype(jnp.bfloat16), "grp", scatter_dimension=0, tiled=True).astype(
            jnp.float32
        ),
    )
    grad_total, moment_rows = lax.psum((group_sum, group_moment), "dp")
    moment_total = moment_rows[0]
    grad_mean = (grad_total / images_all).astype(jnp.bfloat16)
    eigen_out = moment_total / (images_all * side * side)
    width = channels // replicas
    offset = lax.axis_index("dp") * width
    columns = lax.dynamic_slice_in_dim(grad_mean, offset, width, 1)
    rotated = lax.psum_scatter(
        lax.dot_general(
            input_basis, columns, contract_rows, preferred_element_type=jnp.float32
        ).astype(jnp.bfloat16),
        "grp",
        scatter_dimension=0,
        tiled=True,
    ).astype(jnp.float32)
    eigen_cols = lax.dynamic_slice_in_dim(eigen_out, offset, width, 0)
    scaled = (rotated / (input_eigen[:, None] * eigen_cols[None, :] + damping)).astype(jnp.bfloat16)
    back = jnp.dot(
        input_basis,
        lax.all_gather(scaled, "grp", axis=0, tiled=True),
        preferred_element_type=jnp.float32,
    )
    block = back.astype(jnp.bfloat16)
    out_rows = lax.dynamic_slice_in_dim(output_basis, offset, width, 0)
    final = lax.dot_general(
        lax.all_gather(block, "dp", axis=1, tiled=True),
        out_rows,
        (((1,), (1,)), ((), ())),
        preferred_element_type=jnp.float32,
    )
    return final.astype(jnp.bfloat16)


def swap(value, bit):
    return lax.ppermute(value, "dp", [(i, i ^ bit) for i in range(lax.axis_size("dp"))])


def shift(value, step):
    n = lax.axis_size("grp")
    return lax.ppermute(value, "grp", [(i, (i + step) % n) for i in range(n)])


ROUTES = (((1, 3), (0, 2)), ((2, 3), (0, 1)))
ORDER = tuple(
    (2 * chunk + route, flip)
    for chunk in (0, 1)
    for route in (0, 1)
    for flips in ROUTES[route]
    for flip in flips
)


def gradient(lhs, acts, pieces, edge, rows):
    channels = acts.shape[1]
    height = lhs.shape[0] // 3
    size = pieces[0].shape[0]
    for step in range(3):
        window = acts[edge * step : edge * step + 2 * rows, :]
        out = jnp.dot(lhs[...], window, preferred_element_type=F32)
        for tap in range(3):
            column = (3 * step + tap) * channels
            for at, ref in enumerate(pieces):
                start = tap * height + at * size
                ref[:, column : column + channels] = out[start : start + size, :].astype(BF)


def first_kernel(act_a, act_b, dout_a, dout_b, turn, *refs):
    pieces, squared, (acts, later, flipped, turned, lhs) = refs[:4], refs[4], refs[5:]
    rows, channels = act_a.shape
    edge = rows // 16
    images = edge // 16
    half = channels // 2
    sub = half // len(ORDER)
    me = lax.axis_index("dp")
    quarter = me >> 1
    flipped[...] = turn[:, pl.ds(pl.multiple_of((me & 1) * half, half), half)].T
    for at, (part, flip) in enumerate(ORDER):
        start = pl.multiple_of((quarter ^ flip) * 4 * sub + part * sub, sub)
        turned[at * sub : (at + 1) * sub, :] = flipped[pl.ds(start, sub), :]
    acts[0:edge, :] = jnp.zeros((edge, channels), BF)
    acts[edge + 2 * rows :, :] = jnp.zeros((edge, channels), BF)
    acts[edge : edge + rows, :] = act_a[...]
    acts[edge + rows : edge + 2 * rows, :] = act_b[...]
    squares = jnp.zeros((half, 128), F32)
    height = half // 2
    for at, ref in enumerate((dout_a, dout_b)):
        part = lax.dot_general(
            turned[...], ref[...], (((1,), (1,)), ((), ())), preferred_element_type=F32
        )
        for lane in range(0, rows, 128):
            squares = squares + part[:, lane : lane + 128] * part[:, lane : lane + 128]
        for tap, by in enumerate((rows - images, 0, images)):
            moved = (pltpu.roll(part, by, 1) if by else part).astype(BF)
            span = slice(at * rows, (at + 1) * rows)
            lhs[tap * height : (tap + 1) * height, span] = moved[:height, :]
            later[tap * height : (tap + 1) * height, span] = moved[height:, :]
    for at, ref in enumerate(pieces):
        size = ref.shape[0]
        ref[:, 9 * channels :] = squares[at * size : (at + 1) * size, :].astype(BF)
    squared[...] = squares[height:, :].astype(BF)
    gradient(lhs, acts, pieces, edge, rows)


def second_kernel(acts, later, squared, *pieces):
    channels = acts.shape[1]
    rows = later.shape[1] // 2
    for at, ref in enumerate(pieces):
        size = ref.shape[0]
        ref[:, 9 * channels :] = squared[at * size : (at + 1) * size, :]
    gradient(later, acts, pieces, rows // 16, rows)


def grad_parts(act_a, act_b, dout_a, dout_b, turn):
    rows, channels = act_a.shape
    half = channels // 2
    near = pl.BlockSpec(memory_space=pltpu.VMEM)
    piece = jax.ShapeDtypeStruct((half // 8, 9 * channels + 128), BF)
    params = pltpu.CompilerParams(vmem_limit_bytes=12 << 20)
    *first, squared, acts, later = pl.pallas_call(
        first_kernel,
        in_specs=[near] * 5,
        out_specs=[near] * 7,
        out_shape=[piece] * 4
        + [
            jax.ShapeDtypeStruct((half // 2, 128), BF),
            jax.ShapeDtypeStruct((2 * rows + rows // 8, channels), BF),
            jax.ShapeDtypeStruct((3 * half // 2, 2 * rows), BF),
        ],
        scratch_shapes=[
            pltpu.VMEM((half, channels), BF),
            pltpu.VMEM((half, channels), BF),
            pltpu.VMEM((3 * half // 2, 2 * rows), BF),
        ],
        compiler_params=params,
    )(act_a, act_b, dout_a, dout_b, turn)
    second = pl.pallas_call(
        second_kernel,
        in_specs=[near] * 3,
        out_specs=[near] * 4,
        out_shape=[piece] * 4,
        compiler_params=params,
        cost_estimate=pl.CostEstimate(
            flops=9 * channels * channels * rows, bytes_accessed=0, transcendentals=0
        ),
    )(acts, later, squared)
    return [*first, *second]


def map_rows(images):
    h, w, n, c = images.shape
    rows = images.reshape(h, w * n, c)
    return jnp.pad(rows, ((0, 16 - h), (0, (16 - w) * n), (0, 0))).reshape(256 * n, c)


def fetch_kernel(*refs):
    count = len(refs) // 2
    sems = refs[-1]
    copies = [
        pltpu.make_async_copy(refs[at], refs[count + at], sems.at[at]) for at in range(count)
    ]
    for copy in copies:
        copy.start()
    for copy in copies:
        copy.wait()


def fetch(values):
    anywhere = pl.BlockSpec(memory_space=pl.ANY)
    return pl.pallas_call(
        fetch_kernel,
        in_specs=[anywhere] * len(values),
        out_specs=[anywhere] * len(values),
        out_shape=[pltpu.VMEM(value.shape, value.dtype) for value in values],
        scratch_shapes=[pltpu.SemaphoreType.DMA((len(values),))],
        compiler_params=pltpu.CompilerParams(vmem_limit_bytes=56 << 20),
    )(*values)


def load_kernel(source, after, target, sems):
    del after
    rows = source.shape[0] // LOADS
    copies = [
        pltpu.make_async_copy(
            source.at[pl.ds(at * rows, rows)], target.at[pl.ds(at * rows, rows)], sems.at[at]
        )
        for at in range(LOADS)
    ]
    for copy in copies:
        copy.start()
    for copy in copies:
        copy.wait()


def load(value, after):
    return pl.pallas_call(
        load_kernel,
        in_specs=[pl.BlockSpec(memory_space=pl.ANY), pl.BlockSpec(memory_space=pltpu.VMEM)],
        out_specs=pl.BlockSpec(memory_space=pl.ANY),
        out_shape=pltpu.VMEM(value.shape, value.dtype),
        scratch_shapes=[pltpu.SemaphoreType.DMA((LOADS,))],
        compiler_params=pltpu.CompilerParams(vmem_limit_bytes=44 << 20),
        cost_estimate=pl.CostEstimate(flops=0, bytes_accessed=4 * value.size, transcendentals=0),
    )(value, after)


def stage(kernel, out_shape, operands, after=(), flops=0):
    near = pl.BlockSpec(memory_space=pltpu.VMEM)

    def body(*refs):
        kernel(refs[: len(operands)], refs[len(operands) + len(after) :])

    results = pl.pallas_call(
        body,
        in_specs=[near] * (len(operands) + len(after)),
        out_specs=[near] * len(out_shape),
        out_shape=out_shape,
        compiler_params=pltpu.CompilerParams(vmem_limit_bytes=8 << 20),
        cost_estimate=pl.CostEstimate(flops=flops, bytes_accessed=0, transcendentals=0),
    )(*operands, *after)
    return list(results)


def first_sum(ins, outs):
    kept, sent = outs[0], outs[1:]
    sub = sent[0].shape[0]
    for route in (0, 1):
        mine, came = ins[2 * route], ins[2 * route + 1]
        low, high = slice(0, sub), slice(sub, 2 * sub)
        kept[route * sub : (route + 1) * sub, :] = mine[low, :].astype(F32) + came[low, :].astype(
            F32
        )
        sent[route][...] = (mine[high, :].astype(F32) + came[high, :].astype(F32)).astype(BF)


def second_sum(ins, outs):
    *outs, total = outs
    kept, came_a, came_b = ins
    sub = came_a.shape[0]
    for route, came in enumerate((came_a, came_b)):
        rows = slice(route * sub, (route + 1) * sub)
        total[rows, :] = kept[rows, :] + came[...].astype(F32)
    width = outs[0].shape[1] - 128
    me = lax.axis_index("grp")
    groups = len(outs)
    rest = total[:, groups * width :]
    for step, out in enumerate(outs):
        at = pl.multiple_of(lax.rem(me + step, groups) * width, 128)
        out[:, 0:width] = total[:, pl.ds(at, width)].astype(out.dtype)
        out[:, width:] = rest.astype(out.dtype)


def gathered(ins):
    total = ins[0][...]
    for other in ins[1:]:
        total = total + other[...].astype(F32)
    return total


def prepare(ins, outs, images_all, groups):
    columns, moments = outs
    low, rows = columns.shape
    sums = gathered(ins[len(ins) - groups :])
    low -= sums.shape[0]
    for ref, earlier in zip(outs, ins[: len(ins) - groups]):
        ref[:low, :] = earlier[...]
    columns[low:, :] = (sums[:, :rows] / images_all).astype(BF)
    moments[low:, :] = sums[:, rows:]


def rotate(ins, outs, spans):
    columns, basis = ins
    me = lax.axis_index("grp")
    rows = basis.shape[0]
    groups = len(outs) // len(spans)
    for step in range(groups):
        at = pl.multiple_of(lax.rem(me + step, groups) * rows, 128)
        part = jnp.dot(columns[...], basis[:, pl.ds(at, rows)], preferred_element_type=F32)
        for c, (low, high) in enumerate(spans):
            out = outs[groups * c + step]
            out[...] = part[:, low:high].astype(BF).astype(out.dtype)


def rescale(ins, outs, positions, offset):
    *ins, moments, input_eigen = ins
    eigen_out = jnp.sum(moments[...], axis=1, keepdims=True) / positions
    chunk = outs[0].shape[1]
    scale = input_eigen[:, offset : offset + chunk] * eigen_out + damping
    outs[0][...] = (gathered(ins) / scale).astype(BF)


def turn_back(ins, outs):
    *near, weights = ins
    width = near[0].shape[0]
    total = None
    for at, block in enumerate(near):
        part = jnp.dot(
            weights[:, at * width : (at + 1) * width], block[...], preferred_element_type=F32
        )
        total = part if total is None else total + part
    outs[0][...] = total[:width]
    outs[1][...] = total[width:]


def merge(ins, outs):
    outs[0][...] = (ins[0][...] + ins[1][...]).astype(BF)


def restore(ins, outs, steps, offset, last):
    *blocks, basis = ins
    me = lax.axis_index("grp")
    rows = basis.shape[0]
    groups = basis.shape[1] // rows
    total = None
    if len(blocks) > len(steps):
        total = blocks.pop()[...]
    for step, block in zip(steps, blocks):
        chunk = block.shape[1]
        at = pl.multiple_of(lax.rem(me - step + groups, groups) * rows + offset, 128)
        part = lax.dot_general(
            block[...],
            basis[:, pl.ds(at, chunk)],
            (((1,), (1,)), ((), ())),
            preferred_element_type=F32,
        )
        total = part if total is None else total + part
    outs[0][...] = total.astype(outs[0].dtype)


def cube(activations, out_grads, input_basis, output_basis, input_eigen):
    channels = output_basis.shape[0]
    local_images, side = activations.shape[:2]
    images_all = local_images * lax.axis_size("dp") * lax.axis_size("grp")
    groups = lax.axis_size("grp")
    me = lax.axis_index("dp")
    width = channels // 8
    own_rows = input_eigen.shape[0]
    block = (me & 1) * 4 + (me >> 1)

    act_own = activations.transpose(1, 2, 0, 3)
    dout_own = out_grads.transpose(1, 2, 0, 3)
    act_near, dout_near, basis_near = fetch([act_own, dout_own, output_basis])
    act_rows = [map_rows(act_near), map_rows(swap(act_own, 1))]
    dout_rows = [map_rows(dout_near), map_rows(swap(dout_own, 1))]
    both = jnp.concatenate(
        [lax.dynamic_slice_in_dim(basis_near, r * width, width, 0) for r in (me, me ^ 1)], 0
    )
    weights = jnp.concatenate(
        [
            lax.dynamic_slice_in_dim(both, (block ^ flip) * width, width, 1)
            for flip in range(4)
        ],
        1,
    )

    parts = list(grad_parts(*act_rows, *dout_rows, basis_near))

    sub = width // 4
    wide = groups * own_rows + 128
    like = jax.ShapeDtypeStruct
    grp_types = [F32] + [BF] * (groups - 1)
    parts[1], weights = lax.optimization_barrier((parts[1], weights))
    came = [
        [parts[4 * c + 1], swap(parts[4 * c], 2), parts[4 * c + 3], swap(parts[4 * c + 2], 4)]
        for c in (0, 1)
    ]
    basis = load(input_basis, parts[0])
    sums = ()
    for c in (0, 1):
        shapes = [like((2 * sub, wide), F32)] + [like((sub, wide), BF)] * 2
        kept, s_a, s_b = sums = stage(first_sum, shapes, came[c], sums[1:2], WORK[0][c])
        came[c] = [kept, swap(s_a, 4), swap(s_b, 2)]
    held = []
    for c in (0, 1):
        shapes = [like((2 * sub, own_rows + 128), t) for t in grp_types] + [like((2 * sub, wide), F32)]
        own, *others = stage(second_sum, shapes, came[c], (), WORK[7][c])[:groups]
        came[c] = [own] + [shift(value, step + 1) for step, value in enumerate(others)]
    for c in (0, 1):
        rows = 2 * sub * (c + 1)
        held = stage(
            functools.partial(prepare, images_all=images_all, groups=groups),
            [like((rows, own_rows), BF), like((rows, 128), F32)],
            held + came[c],
            (),
            WORK[8][c],
        )
    columns, moments = held

    spans = ((0, own_rows // 128 // 2 * 128), (own_rows // 128 // 2 * 128, own_rows))
    eigen_row = input_eigen.reshape(1, own_rows)
    rotated = stage(
        functools.partial(rotate, spans=spans),
        [like((width, high - low), t) for low, high in spans for t in grp_types],
        [columns, basis],
        (),
        WORK[2][0],
    )
    came = []
    for c in (0, 1):
        own, *others = rotated[groups * c : groups * (c + 1)]
        came.append([own] + [shift(value, step + 1) for step, value in enumerate(others)])
    near, scaled = [], ()
    for (low, high), values in zip(spans, came):
        scaled = stage(
            functools.partial(rescale, positions=images_all * side * side, offset=low),
            [like((width, high - low), BF)],
            values + [moments, eigen_row],
            scaled,
            WORK[3][low > 0],
        )
        near.append(scaled + [swap(scaled[0], bit) for bit in (2, 4, 6)])
    held = []
    for (low, high), values in zip(spans, near):
        mine, sent = stage(
            turn_back,
            [like((width, high - low), F32)] * 2,
            values + [weights],
            (),
            WORK[4][low > 0],
        )
        (own,) = stage(merge, [like((width, high - low), BF)], [mine, swap(sent, 1)], (), WORK[5][low > 0])
        held.append([own] + [shift(own, step) for step in range(1, groups)])

    update = []
    calls = [(0, (0,)), (1, (0,)), (0, tuple(range(1, groups)))]
    calls += [(1, (step,)) for step in range(1, groups)]
    for at, (c, steps) in enumerate(calls):
        last = at == len(calls) - 1
        update = stage(
            functools.partial(restore, steps=steps, offset=spans[c][0], last=last),
            [like((width, own_rows), BF) if last else like((width, own_rows), F32)],
            [held[c][step] for step in steps] + update + [basis],
            (),
            len(steps) * WORK[6][c],
        )
    return update[0].T


def solution(mesh):
    in_specs = (
        P(("dp", "grp"), None, None, None),
        P(("dp", "grp"), None, None, None),
        P("grp", None),
        P(),
        P("grp"),
    )
    out_specs = P("grp", "dp")
    plan = cube if mesh.shape["dp"] == 8 else any_mesh
    return jax.shard_map(plan, mesh=mesh, in_specs=in_specs, out_specs=out_specs, check_vma=False)
```

```python
import functools

import jax
import jax.numpy as jnp
from jax import lax
from jax.experimental import pallas as pl
from jax.experimental.pallas import tpu as pltpu
from jax.sharding import PartitionSpec as P

damping = 1.0
BF = jnp.bfloat16
F32 = jnp.float32
WORK = [[0, 0], [400000000, 1000000000], [75000000, 75000000], [400000000, 0], [30000000, 150000000], [0, 0], [1000000000, 100000000], [0, 0], [300000000, 0]]
LOADS = 8


def unfold(images):
    side = images.shape[1]
    channels = images.shape[3]
    padded = jnp.pad(images, ((0, 0), (1, 1), (1, 1), (0, 0)))
    pieces = [
        padded[:, row : row + side, col : col + side, :] for row in range(3) for col in range(3)
    ]
    return jnp.concatenate(pieces, axis=-1).reshape(-1, 9 * channels)


def rounded(value):
    return lax.optimization_barrier(value.astype(jnp.bfloat16)).astype(jnp.float32)


def any_mesh(activations, out_grads, input_basis, output_basis, input_eigen):
    channels = output_basis.shape[0]
    side = activations.shape[1]
    local_images = activations.shape[0]
    replicas = lax.axis_size("dp")
    groups = lax.axis_size("grp")
    images_all = local_images * replicas * groups
    contract_rows = (((0,), (0,)), ((), ()))
    flat = out_grads.reshape(-1, channels)
    turned = jnp.dot(flat, output_basis, preferred_element_type=jnp.float32)
    turned_b = turned.astype(jnp.bfloat16)
    moment = rounded(jnp.sum(turned * turned, axis=0))
    patches = unfold(activations)
    term = lax.dot_general(patches, turned_b, contract_rows, preferred_element_type=jnp.float32)
    tiled = jnp.broadcast_to(moment[None, :], (groups, channels))
    group_sum, group_moment = (
        lax.psum_scatter(term.astype(jnp.bfloat16), "grp", scatter_dimension=0, tiled=True).astype(
            jnp.float32
        ),
        lax.psum_scatter(tiled.astype(jnp.bfloat16), "grp", scatter_dimension=0, tiled=True).astype(
            jnp.float32
        ),
    )
    grad_total, moment_rows = lax.psum((group_sum, group_moment), "dp")
    moment_total = moment_rows[0]
    grad_mean = (grad_total / images_all).astype(jnp.bfloat16)
    eigen_out = moment_total / (images_all * side * side)
    width = channels // replicas
    offset = lax.axis_index("dp") * width
    columns = lax.dynamic_slice_in_dim(grad_mean, offset, width, 1)
    rotated = lax.psum_scatter(
        lax.dot_general(
            input_basis, columns, contract_rows, preferred_element_type=jnp.float32
        ).astype(jnp.bfloat16),
        "grp",
        scatter_dimension=0,
        tiled=True,
    ).astype(jnp.float32)
    eigen_cols = lax.dynamic_slice_in_dim(eigen_out, offset, width, 0)
    scaled = (rotated / (input_eigen[:, None] * eigen_cols[None, :] + damping)).astype(jnp.bfloat16)
    back = jnp.dot(
        input_basis,
        lax.all_gather(scaled, "grp", axis=0, tiled=True),
        preferred_element_type=jnp.float32,
    )
    block = back.astype(jnp.bfloat16)
    out_rows = lax.dynamic_slice_in_dim(output_basis, offset, width, 0)
    final = lax.dot_general(
        lax.all_gather(block, "dp", axis=1, tiled=True),
        out_rows,
        (((1,), (1,)), ((), ())),
        preferred_element_type=jnp.float32,
    )
    return final.astype(jnp.bfloat16)


def swap(value, bit):
    return lax.ppermute(value, "dp", [(i, i ^ bit) for i in range(lax.axis_size("dp"))])


def shift(value, step):
    n = lax.axis_size("grp")
    return lax.ppermute(value, "grp", [(i, (i + step) % n) for i in range(n)])


ROUTES = (((1, 3), (0, 2)), ((2, 3), (0, 1)))
ORDER = tuple(
    (2 * chunk + route, flip)
    for chunk in (0, 1)
    for route in (0, 1)
    for flips in ROUTES[route]
    for flip in flips
)


def gradient(lhs, acts, pieces, edge, rows):
    channels = acts.shape[1]
    height = lhs.shape[0] // 3
    size = pieces[0].shape[0]
    for step in range(3):
        window = acts[edge * step : edge * step + 2 * rows, :]
        out = jnp.dot(lhs[...], window, preferred_element_type=F32)
        for tap in range(3):
            column = (3 * step + tap) * channels
            for at, ref in enumerate(pieces):
                start = tap * height + at * size
                ref[:, column : column + channels] = out[start : start + size, :].astype(BF)


def first_kernel(act_a, act_b, dout_a, dout_b, turn, *refs):
    pieces, squared, (acts, later, flipped, turned, lhs) = refs[:4], refs[4], refs[5:]
    rows, channels = act_a.shape
    edge = rows // 16
    images = edge // 16
    half = channels // 2
    sub = half // len(ORDER)
    me = lax.axis_index("dp")
    quarter = me >> 1
    flipped[...] = turn[:, pl.ds(pl.multiple_of((me & 1) * half, half), half)].T
    for at, (part, flip) in enumerate(ORDER):
        start = pl.multiple_of((quarter ^ flip) * 4 * sub + part * sub, sub)
        turned[at * sub : (at + 1) * sub, :] = flipped[pl.ds(start, sub), :]
    acts[0:edge, :] = jnp.zeros((edge, channels), BF)
    acts[edge + 2 * rows :, :] = jnp.zeros((edge, channels), BF)
    acts[edge : edge + rows, :] = act_a[...]
    acts[edge + rows : edge + 2 * rows, :] = act_b[...]
    squares = jnp.zeros((half, 128), F32)
    height = half // 2
    for at, ref in enumerate((dout_a, dout_b)):
        part = lax.dot_general(
            turned[...], ref[...], (((1,), (1,)), ((), ())), preferred_element_type=F32
        )
        for lane in range(0, rows, 128):
            squares = squares + part[:, lane : lane + 128] * part[:, lane : lane + 128]
        for tap, by in enumerate((rows - images, 0, images)):
            moved = (pltpu.roll(part, by, 1) if by else part).astype(BF)
            span = slice(at * rows, (at + 1) * rows)
            lhs[tap * height : (tap + 1) * height, span] = moved[:height, :]
            later[tap * height : (tap + 1) * height, span] = moved[height:, :]
    for at, ref in enumerate(pieces):
        size = ref.shape[0]
        ref[:, 9 * channels :] = squares[at * size : (at + 1) * size, :].astype(BF)
    squared[...] = squares[height:, :].astype(BF)
    gradient(lhs, acts, pieces, edge, rows)


def second_kernel(acts, later, squared, *pieces):
    channels = acts.shape[1]
    rows = later.shape[1] // 2
    for at, ref in enumerate(pieces):
        size = ref.shape[0]
        ref[:, 9 * channels :] = squared[at * size : (at + 1) * size, :]
    gradient(later, acts, pieces, rows // 16, rows)


def grad_parts(act_a, act_b, dout_a, dout_b, turn):
    rows, channels = act_a.shape
    half = channels // 2
    near = pl.BlockSpec(memory_space=pltpu.VMEM)
    piece = jax.ShapeDtypeStruct((half // 8, 9 * channels + 128), BF)
    params = pltpu.CompilerParams(vmem_limit_bytes=12 << 20)
    *first, squared, acts, later = pl.pallas_call(
        first_kernel,
        in_specs=[near] * 5,
        out_specs=[near] * 7,
        out_shape=[piece] * 4
        + [
            jax.ShapeDtypeStruct((half // 2, 128), BF),
            jax.ShapeDtypeStruct((2 * rows + rows // 8, channels), BF),
            jax.ShapeDtypeStruct((3 * half // 2, 2 * rows), BF),
        ],
        scratch_shapes=[
            pltpu.VMEM((half, channels), BF),
            pltpu.VMEM((half, channels), BF),
            pltpu.VMEM((3 * half // 2, 2 * rows), BF),
        ],
        compiler_params=params,
    )(act_a, act_b, dout_a, dout_b, turn)
    second = pl.pallas_call(
        second_kernel,
        in_specs=[near] * 3,
        out_specs=[near] * 4,
        out_shape=[piece] * 4,
        compiler_params=params,
        cost_estimate=pl.CostEstimate(
            flops=9 * channels * channels * rows, bytes_accessed=0, transcendentals=0
        ),
    )(acts, later, squared)
    return [*first, *second]


def map_rows(images):
    h, w, n, c = images.shape
    rows = images.reshape(h, w * n, c)
    return jnp.pad(rows, ((0, 16 - h), (0, (16 - w) * n), (0, 0))).reshape(256 * n, c)


def fetch_kernel(*refs):
    count = len(refs) // 2
    sems = refs[-1]
    copies = [
        pltpu.make_async_copy(refs[at], refs[count + at], sems.at[at]) for at in range(count)
    ]
    for copy in copies:
        copy.start()
    for copy in copies:
        copy.wait()


def fetch(values):
    anywhere = pl.BlockSpec(memory_space=pl.ANY)
    return pl.pallas_call(
        fetch_kernel,
        in_specs=[anywhere] * len(values),
        out_specs=[anywhere] * len(values),
        out_shape=[pltpu.VMEM(value.shape, value.dtype) for value in values],
        scratch_shapes=[pltpu.SemaphoreType.DMA((len(values),))],
        compiler_params=pltpu.CompilerParams(vmem_limit_bytes=56 << 20),
    )(*values)


def load_kernel(source, after, target, sems):
    del after
    rows = source.shape[0] // LOADS
    copies = [
        pltpu.make_async_copy(
            source.at[pl.ds(at * rows, rows)], target.at[pl.ds(at * rows, rows)], sems.at[at]
        )
        for at in range(LOADS)
    ]
    for copy in copies:
        copy.start()
    for copy in copies:
        copy.wait()


def load(value, after):
    return pl.pallas_call(
        load_kernel,
        in_specs=[pl.BlockSpec(memory_space=pl.ANY), pl.BlockSpec(memory_space=pltpu.VMEM)],
        out_specs=pl.BlockSpec(memory_space=pl.ANY),
        out_shape=pltpu.VMEM(value.shape, value.dtype),
        scratch_shapes=[pltpu.SemaphoreType.DMA((LOADS,))],
        compiler_params=pltpu.CompilerParams(vmem_limit_bytes=44 << 20),
        cost_estimate=pl.CostEstimate(flops=0, bytes_accessed=4 * value.size, transcendentals=0),
    )(value, after)


def stage(kernel, out_shape, operands, after=(), flops=0):
    near = pl.BlockSpec(memory_space=pltpu.VMEM)

    def body(*refs):
        kernel(refs[: len(operands)], refs[len(operands) + len(after) :])

    results = pl.pallas_call(
        body,
        in_specs=[near] * (len(operands) + len(after)),
        out_specs=[near] * len(out_shape),
        out_shape=out_shape,
        compiler_params=pltpu.CompilerParams(vmem_limit_bytes=8 << 20),
        cost_estimate=pl.CostEstimate(flops=flops, bytes_accessed=0, transcendentals=0),
    )(*operands, *after)
    return list(results)


def first_sum(ins, outs):
    kept, sent = outs[0], outs[1:]
    sub = sent[0].shape[0]
    for route in (0, 1):
        mine, came = ins[2 * route], ins[2 * route + 1]
        low, high = slice(0, sub), slice(sub, 2 * sub)
        kept[route * sub : (route + 1) * sub, :] = mine[low, :].astype(F32) + came[low, :].astype(
            F32
        )
        sent[route][...] = (mine[high, :].astype(F32) + came[high, :].astype(F32)).astype(BF)


def second_sum(ins, outs):
    kept, *others = ins
    sub = others[0].shape[0]
    width = outs[0].shape[1] - 128
    me = lax.axis_index("grp")
    groups = len(outs)
    for route, came in enumerate(others):
        rows = slice(route * sub, (route + 1) * sub)
        end = groups * width
        rest = kept[rows, end:] + came[:, end:].astype(F32)
        for step, out in enumerate(outs):
            span = pl.ds(pl.multiple_of(lax.rem(me + step, groups) * width, 128), width)
            block = kept[rows, span] + came[:, span].astype(F32)
            out[rows, 0:width] = block.astype(out.dtype)
            out[rows, width:] = rest.astype(out.dtype)


def gathered(ins):
    total = ins[0][...]
    for other in ins[1:]:
        total = total + other[...].astype(F32)
    return total


def prepare(ins, outs, images_all, groups):
    columns, moments = outs
    low, rows = columns.shape
    sums = gathered(ins[len(ins) - groups :])
    low -= sums.shape[0]
    for ref, earlier in zip(outs, ins[: len(ins) - groups]):
        ref[:low, :] = earlier[...]
    columns[low:, :] = (sums[:, :rows] / images_all).astype(BF)
    moments[low:, :] = sums[:, rows:]


def rotate(ins, outs, spans):
    columns, basis = ins
    me = lax.axis_index("grp")
    rows = basis.shape[0]
    groups = len(outs) // len(spans)
    for step in range(groups):
        at = pl.multiple_of(lax.rem(me + step, groups) * rows, 128)
        part = jnp.dot(columns[...], basis[:, pl.ds(at, rows)], preferred_element_type=F32)
        for c, (low, high) in enumerate(spans):
            out = outs[groups * c + step]
            out[...] = part[:, low:high].astype(BF).astype(out.dtype)


def rescale(ins, outs, positions, offset):
    *ins, moments, input_eigen = ins
    eigen_out = jnp.sum(moments[...], axis=1, keepdims=True) / positions
    chunk = outs[0].shape[1]
    scale = input_eigen[:, offset : offset + chunk] * eigen_out + damping
    outs[0][...] = (gathered(ins) / scale).astype(BF)


def turn_back(ins, outs):
    *near, weights = ins
    width = near[0].shape[0]
    total = None
    for at, block in enumerate(near):
        part = jnp.dot(
            weights[:, at * width : (at + 1) * width], block[...], preferred_element_type=F32
        )
        total = part if total is None else total + part
    outs[0][...] = total[:width]
    outs[1][...] = total[width:]


def merge(ins, outs):
    outs[0][...] = (ins[0][...] + ins[1][...]).astype(BF)


def restore(ins, outs, steps, offset, last):
    *blocks, basis = ins
    me = lax.axis_index("grp")
    rows = basis.shape[0]
    groups = basis.shape[1] // rows
    total = None
    if len(blocks) > len(steps):
        total = blocks.pop()[...]
    for step, block in zip(steps, blocks):
        chunk = block.shape[1]
        at = pl.multiple_of(lax.rem(me - step + groups, groups) * rows + offset, 128)
        part = lax.dot_general(
            block[...],
            basis[:, pl.ds(at, chunk)],
            (((1,), (1,)), ((), ())),
            preferred_element_type=F32,
        )
        total = part if total is None else total + part
    outs[0][...] = total.astype(outs[0].dtype)


def cube(activations, out_grads, input_basis, output_basis, input_eigen):
    channels = output_basis.shape[0]
    local_images, side = activations.shape[:2]
    images_all = local_images * lax.axis_size("dp") * lax.axis_size("grp")
    groups = lax.axis_size("grp")
    me = lax.axis_index("dp")
    width = channels // 8
    own_rows = input_eigen.shape[0]
    block = (me & 1) * 4 + (me >> 1)

    act_own = activations.transpose(1, 2, 0, 3)
    dout_own = out_grads.transpose(1, 2, 0, 3)
    act_near, dout_near, basis_near = fetch([act_own, dout_own, output_basis])
    act_rows = [map_rows(act_near), map_rows(swap(act_own, 1))]
    dout_rows = [map_rows(dout_near), map_rows(swap(dout_own, 1))]
    both = jnp.concatenate(
        [lax.dynamic_slice_in_dim(basis_near, r * width, width, 0) for r in (me, me ^ 1)], 0
    )
    weights = jnp.concatenate(
        [
            lax.dynamic_slice_in_dim(both, (block ^ flip) * width, width, 1)
            for flip in range(4)
        ],
        1,
    )

    parts = list(grad_parts(*act_rows, *dout_rows, basis_near))

    sub = width // 4
    wide = groups * own_rows + 128
    like = jax.ShapeDtypeStruct
    grp_types = [F32] + [BF] * (groups - 1)
    parts[1], weights = lax.optimization_barrier((parts[1], weights))
    came = [
        [parts[4 * c + 1], swap(parts[4 * c], 2), parts[4 * c + 3], swap(parts[4 * c + 2], 4)]
        for c in (0, 1)
    ]
    basis = load(input_basis, parts[0])
    sums = ()
    for c in (0, 1):
        shapes = [like((2 * sub, wide), F32)] + [like((sub, wide), BF)] * 2
        kept, s_a, s_b = sums = stage(first_sum, shapes, came[c], sums[1:2], WORK[0][c])
        came[c] = [kept, swap(s_a, 4), swap(s_b, 2)]
    held = []
    for c in (0, 1):
        shapes = [like((2 * sub, own_rows + 128), t) for t in grp_types]
        own, *others = stage(second_sum, shapes, came[c], (), WORK[7][c])
        came[c] = [own] + [shift(value, step + 1) for step, value in enumerate(others)]
    for c in (0, 1):
        rows = 2 * sub * (c + 1)
        held = stage(
            functools.partial(prepare, images_all=images_all, groups=groups),
            [like((rows, own_rows), BF), like((rows, 128), F32)],
            held + came[c],
            (),
            WORK[8][c],
        )
    columns, moments = held

    spans = ((0, own_rows // 128 // 2 * 128), (own_rows // 128 // 2 * 128, own_rows))
    eigen_row = input_eigen.reshape(1, own_rows)
    rotated = stage(
        functools.partial(rotate, spans=spans),
        [like((width, high - low), t) for low, high in spans for t in grp_types],
        [columns, basis],
        (),
        WORK[2][0],
    )
    came = []
    for c in (0, 1):
        own, *others = rotated[groups * c : groups * (c + 1)]
        came.append([own] + [shift(value, step + 1) for step, value in enumerate(others)])
    near, scaled = [], ()
    for (low, high), values in zip(spans, came):
        scaled = stage(
            functools.partial(rescale, positions=images_all * side * side, offset=low),
            [like((width, high - low), BF)],
            values + [moments, eigen_row],
            scaled,
            WORK[3][low > 0],
        )
        near.append(scaled + [swap(scaled[0], bit) for bit in (2, 4, 6)])
    held = []
    for (low, high), values in zip(spans, near):
        mine, sent = stage(
            turn_back,
            [like((width, high - low), F32)] * 2,
            values + [weights],
            (),
            WORK[4][low > 0],
        )
        (own,) = stage(merge, [like((width, high - low), BF)], [mine, swap(sent, 1)], (), WORK[5][low > 0])
        held.append([own] + [shift(own, step) for step in range(1, groups)])

    update = []
    calls = [(0, (0,)), (1, (0,)), (0, tuple(range(1, groups)))]
    calls += [(1, (step,)) for step in range(1, groups)]
    for at, (c, steps) in enumerate(calls):
        last = at == len(calls) - 1
        update = stage(
            functools.partial(restore, steps=steps, offset=spans[c][0], last=last),
            [like((width, own_rows), BF) if last else like((width, own_rows), F32)],
            [held[c][step] for step in steps] + update + [basis],
            (),
            len(steps) * WORK[6][c],
        )
    return update[0].T


def solution(mesh):
    in_specs = (
        P(("dp", "grp"), None, None, None),
        P(("dp", "grp"), None, None, None),
        P("grp", None),
        P(),
        P("grp"),
    )
    out_specs = P("grp", "dp")
    plan = cube if mesh.shape["dp"] == 8 else any_mesh
    return jax.shard_map(plan, mesh=mesh, in_specs=in_specs, out_specs=out_specs, check_vma=False)
```
